128 devices in a mesh: chan: 32 (over x, y, z_lo), tm: 4 (over z_hi, core).
Axes of the slice: x: 4, y: 4, z: 4 (z_hi: 2, z_lo: 2; z = z_hi * 2 + z_lo), core: 2. Of those that a mesh axis runs over, the one named last changes fastest.
Arguments:
- spectra: bfloat16 [256, 2, 250, 8192], P('tm', None, None, 'chan'), may hold values from -6 to 6
- src_blocks: int32 [2], replicated, may hold values from 0 to 127
- valid: int32 [256], P('tm'), may hold values 0 or 1
Outputs:
- stacked: bfloat16 [128, 101, 8192], P('tm', None, 'chan')
The draws below stay inside these ranges and needn't reach their ends.
All inputs are finite; a program needn't handle non-finite values. No bound on the sum of `valid` on one device may be relied on, other than what follows from the above.
Results may differ from the reference program's by a relative error of at most 0.013.
Values may be sent and summed in bfloat16 or wider, within the bound.
No kernel may reach another device: no remote copies, remote signals or barrier semaphores. Data moves between devices by JAX's collectives and lax.ppermute only.
A program may use at most 192 MiB of HBM per device.

```python
import jax
import jax.numpy as jnp
from jax import lax

F = 250
LAGS = 101
SRC_BLK = 64
SEG_DEV = 64
CH = 8192
SEGS = 256
SRC = 128
NBLK = 128
N_TM = 4


def touch_ends(entries, stream_key, smallest, largest):
    shape = entries.shape
    spot = [jax.random.randint(jax.random.fold_in(stream_key, axis), (), 0, shape[axis]) for axis in range(len(shape))]
    entries = entries.at[tuple(spot)].set(smallest)
    longest = shape.index(max(shape))
    spot[longest] = (spot[longest] + 1) % shape[longest]
    return entries.at[tuple(spot)].set(largest)


def steps_of(key, shape, split, smallest, top_value):
    factor_of, own = 1.0, jax.random.fold_in(key, 6)
    for axis_at, parts in split:
        draws = jnp.exp(jax.random.uniform(jax.random.fold_in(own, axis_at), (parts,), jnp.float32, smallest / len(split), top_value / len(split)))
        factor_of = factor_of * jnp.repeat(draws, shape[axis_at] // parts).reshape([-1 if axis == axis_at else 1 for axis in range(len(shape))])
    return factor_of


def noise(rng, shape, width, most, cuts=(), kind=jnp.bfloat16):
    level = steps_of(rng, shape, cuts, -0.22, 0.18) if cuts else 1.0
    entries = jax.random.normal(rng, shape, jnp.float32) * width * level
    return jnp.minimum(jnp.maximum(entries, -most), most).astype(kind)


def setup_inputs(seed: int = 0) -> dict:
    key_of = jax.random.split(jax.random.key(seed), 4)
    spectra = noise(key_of[0], (SEGS, 2, F, CH), 1.0, 6.0, ((0, 4), (3, 32)))
    src_blocks = jax.random.randint(key_of[1], (2,), 0, NBLK).astype(jnp.int32)
    valid = touch_ends((jax.random.randint(key_of[2], (SEGS,), 0, 4) < 3).astype(jnp.int32), jax.random.fold_in(key_of[2], 1), 0, 1)
    return dict(spectra=spectra, src_blocks=src_blocks, valid=valid)


def lag_table(bin_count, lag_count, segment_total):
    bins_idx = jnp.arange(bin_count, dtype=jnp.int32) + 1
    lag_steps = jnp.arange(lag_count, dtype=jnp.int32) - (lag_count - 1) // 2
    phase_int = lag_steps[:, None] * bins_idx[None, :] % (2 * bin_count)
    phase = phase_int.astype(jnp.float32) * (2.0 * jnp.pi / (2.0 * bin_count))
    scale = 1.0 / jnp.sqrt(jnp.float32(segment_total * bin_count))
    return jnp.stack([jnp.cos(phase) * scale, -jnp.sin(phase) * scale]).astype(jnp.bfloat16)

def cross_spectra(source, spectra):
    rotated = jnp.concatenate([spectra[:, 1:2], -spectra[:, 0:1]], axis=1)
    source_wide = source.astype(jnp.float32)
    real_part = jnp.einsum('scfk,scfr->fkr', source_wide, spectra.astype(jnp.float32))
    imag_part = jnp.einsum('scfk,scfr->fkr', source_wide, rotated.astype(jnp.float32))
    return jnp.stack([real_part, imag_part]).astype(jnp.bfloat16)

def to_lags(table, cross):
    result = jnp.einsum('plf,pfkr->klr', table.astype(jnp.float32), cross.astype(jnp.float32))
    return result.astype(jnp.bfloat16)

def reference(spectra, src_blocks, valid):
    table = lag_table(F, LAGS, SEGS)
    grouped = spectra.reshape(N_TM, SEG_DEV, 2, F, CH)
    grouped_mask = valid.reshape(N_TM, SEG_DEV)

    def one_group(carry, inputs):
        shard_spec, shard_mask = inputs
        keep_mask = shard_mask.astype(jnp.bfloat16)[:, None, None, None]
        pieces = []
        for block in range(2):
            start = (src_blocks[block] * SRC_BLK).astype(jnp.int32)
            source = lax.dynamic_slice_in_dim(shard_spec, start, SRC_BLK, 3) * keep_mask
            pieces.append(to_lags(table, cross_spectra(source, shard_spec)))
        partial_value = lax.optimization_barrier(jnp.concatenate(pieces, axis=0))
        return (carry + partial_value.astype(jnp.float32), None)
    start_sum = jnp.zeros((SRC, LAGS, CH), jnp.float32)
    total, _ = lax.scan(one_group, start_sum, (grouped, grouped_mask))
    return total.astype(jnp.bfloat16)
```

```python
import jax
import jax.numpy as jnp
from jax import lax
from jax.experimental import pallas as pl
from jax.experimental.pallas import tpu as pltpu
from jax.sharding import PartitionSpec as P

LAGS = 101
SRC_BLK = 64
BINS = 250
CHUNKS = 2
ROWS = 128 // CHUNKS
LAG_PAD = 112


def shift_x(x, step):
    pairs = [((a * 4 + b) * 2 + c, (((a + step) % 4) * 4 + b) * 2 + c) for a in range(4) for b in range(4) for c in range(2)]
    return lax.ppermute(x, "chan", pairs)


def shift_y(x, step):
    pairs = [((a * 4 + b) * 2 + c, (a * 4 + (b + step) % 4) * 2 + c) for a in range(4) for b in range(4) for c in range(2)]
    return lax.ppermute(x, "chan", pairs)


def swap_z(x):
    return lax.ppermute(x, "chan", [(a, a ^ 1) for a in range(32)])


def swap_core(x):
    return lax.ppermute(x, "tm", [(a, a ^ 1) for a in range(4)])


def swap_far(x):
    return lax.ppermute(x, "tm", [(a, a ^ 2) for a in range(4)])


def lag_table(freqs, lag_count, segment_total):
    lag_steps = jnp.arange(lag_count, dtype=jnp.int32) - (LAGS - 1) // 2
    phase_int = lag_steps[:, None] * (freqs + 1)[None, :] % (2 * BINS)
    phase = phase_int.astype(jnp.float32) * (2.0 * jnp.pi / (2.0 * BINS))
    scale = 1.0 / jnp.sqrt(jnp.float32(segment_total * BINS))
    both = jnp.stack([jnp.cos(phase) * scale, -jnp.sin(phase) * scale])
    return jnp.where((freqs < BINS)[None, None, :], both, 0.0).astype(jnp.bfloat16)


def pick_kernel(first_ref, pick_ref, mask_ref, spec_ref, out_ref):
    step = pl.program_id(0)
    for w in range(8):
        rows = lax.dot_general(
            pick_ref[...], spec_ref[w], (((1,), (1,)), ((), ())), preferred_element_type=jnp.float32
        )
        kept = jnp.where((first_ref[0] + step) * 8 + w < BINS, rows * mask_ref[...], 0.0)
        out_ref[w] = kept.astype(jnp.bfloat16)


def pick_rows(first, pick, mask, spec):
    return pl.pallas_call(
        pick_kernel,
        grid_spec=pltpu.PrefetchScalarGridSpec(
            num_scalar_prefetch=1,
            grid=(4,),
            in_specs=[
                pl.BlockSpec((128, 256), lambda i, s: (0, 0)),
                pl.BlockSpec((1, 128), lambda i, s: (0, 0)),
                pl.BlockSpec((8, 128, 256), lambda i, s: (s[0] + i, 0, 0)),
            ],
            out_specs=pl.BlockSpec((8, 128, 128), lambda i, s: (i, 0, 0)),
        ),
        out_shape=jax.ShapeDtypeStruct((32, 128, 128), jnp.bfloat16),
        cost_estimate=pl.CostEstimate(flops=2 * 32 * 128 * 128 * 256, bytes_accessed=3 << 20, transcendentals=0),
        name="pick_rows",
    )(first, pick, mask, spec)


def correlate_kernel(blocks_ref, table_ref, sign_ref, spec_ref, src_ref, send_ref, keep_ref, left, right, acc):
    step = pl.program_id(0)
    base = lax.rem(step, 16) * 8
    for w in range(8):
        rows = src_ref[w]
        turned = jnp.concatenate([rows[:, 64:], rows[:, :64]], axis=1) * sign_ref[...]
        both = jnp.concatenate([rows, turned], axis=0)
        cross = jnp.dot(both, spec_ref[w], preferred_element_type=jnp.float32)
        for part in range(2):
            place = pl.ds(part * 128 + base + w, ROWS, stride=256)
            piece = cross[part * ROWS : (part + 1) * ROWS]
            left[place, :] = piece[:, :128]
            right[place, :] = piece[:, 128:]

    def lags(k):
        rows = pl.ds(pl.multiple_of(k * 256, 256), 256)
        cross = jnp.concatenate(
            [left[rows, :].astype(jnp.bfloat16), right[rows, :].astype(jnp.bfloat16)], axis=1
        )
        return jnp.dot(table_ref[0], cross, preferred_element_type=jnp.float32)

    @pl.when(step == 15)
    def _():
        @pl.loop(0, ROWS)
        def _(k):
            acc[k] = lags(k)

    @pl.when(step == 31)
    def _():
        @pl.loop(0, ROWS // 2)
        def _(k):
            send_ref[k] = (acc[k] + lags(k))[:LAGS].astype(jnp.bfloat16)

        @pl.loop(0, ROWS // 2)
        def _(k):
            high = k + ROWS // 2
            keep_ref[k] = (acc[high] + lags(high))[:LAGS].astype(jnp.bfloat16)


def correlate(blocks, table, sign, spec, src):
    half = jax.ShapeDtypeStruct((ROWS // 2, LAGS, 256), jnp.bfloat16)
    whole = pl.BlockSpec((ROWS // 2, LAGS, 256), lambda i, s: (0, 0, 0))
    return pl.pallas_call(
        correlate_kernel,
        grid_spec=pltpu.PrefetchScalarGridSpec(
            num_scalar_prefetch=1,
            grid=(32,),
            in_specs=[
                pl.BlockSpec((1, LAG_PAD, 256), lambda i, s: (i // 16, 0, 0)),
                pl.BlockSpec((1, 128), lambda i, s: (0, 0)),
                pl.BlockSpec((8, 128, 256), lambda i, s: (s[i], 0, 0)),
                pl.BlockSpec((8, ROWS, 128), lambda i, s: (i, 0, 0)),
            ],
            out_specs=[whole, whole],
            scratch_shapes=[
                pltpu.VMEM((ROWS * 256, 128), jnp.float32),
                pltpu.VMEM((ROWS * 256, 128), jnp.float32),
                pltpu.VMEM((ROWS, LAG_PAD, 256), jnp.float32),
            ],
        ),
        out_shape=[half, half],
        compiler_params=pltpu.CompilerParams(vmem_limit_bytes=44 << 20),
        cost_estimate=pl.CostEstimate(flops=20 * 10**9, bytes_accessed=24 << 20, transcendentals=0),
        name="correlate",
    )(blocks, table, sign, spec, src)


def body(spectra, src_blocks, valid):
    chan_index = lax.axis_index("chan")
    tm_index = lax.axis_index("tm")
    x, y = chan_index // 8, chan_index // 2 % 4
    core, far = tm_index % 2, tm_index // 2

    spec = jnp.transpose(spectra, (2, 1, 0, 3)).reshape(BINS, 128, 256)

    q = jnp.arange(128, dtype=jnp.int32)
    part, group, within = q // ROWS, q % ROWS // (ROWS // 4), q % (ROWS // 4)
    dest_core = jnp.where(group < 2, 1 - core, core)
    dest_far = jnp.where(group % 2 == 0, 1 - far, far)
    row = 32 * (2 * dest_far + dest_core) + (ROWS // 4) * part + within
    block = jnp.where(row < SRC_BLK, src_blocks[0], src_blocks[1])
    channel = block * SRC_BLK + row % SRC_BLK - chan_index * 256
    pick = (channel[:, None] == jnp.arange(256, dtype=jnp.int32)[None, :]).astype(jnp.bfloat16)
    mask = jnp.tile(valid.astype(jnp.float32), 2)[None, :]
    sign = jnp.where(jnp.arange(128) < 64, -1.0, 1.0).astype(jnp.bfloat16)[None, :]

    def scatter_first(base, at, shift):
        own = [pick_rows((base + 4 * ((at + d) % 4))[None], pick, mask, spec) for d in (1, 3, 2, 0)]
        return [own[3]] + [shift(own[i], d) for i, d in enumerate((1, 3, 2))]

    def scatter_second(quarters, at, shift):
        def piece(d):
            cut = [lax.dynamic_slice_in_dim(a, 8 * ((at + d) % 4), 8, 0) for a in quarters]
            return (cut[0] + cut[1]) + (cut[2] + cut[3])

        got = [shift(piece(d), d) for d in (1, 3, 2)]
        return (piece(0) + got[0]) + (got[1] + got[2])

    zero = jnp.int32(0)
    quarters_a = scatter_first(zero, x, shift_x)
    quarters_b = scatter_first(zero + 16, y, shift_y)
    piece_a = scatter_second(quarters_a, y, shift_y)
    piece_b = scatter_second(quarters_b, x, shift_x)
    piece_a = piece_a + swap_z(piece_a)
    piece_b = piece_b + swap_z(piece_b)

    def gather(a, shift):
        got = {d: shift(a, d) for d in (1, 3, 2)}
        return [a, got[1], got[2], got[3]]

    inner_a = gather(piece_a, shift_y)
    inner_b = gather(piece_b, shift_x)

    i = jnp.arange(256, dtype=jnp.int32)
    e, j, w = i % 128 // 32, i % 32 // 8, i % 8
    freqs = jnp.where(
        i < 128, 32 * ((x - e) % 4) + 8 * ((y - j) % 4) + w, 128 + 32 * ((y - e) % 4) + 8 * ((x - j) % 4) + w
    )
    table = lag_table(freqs, LAG_PAD, 256).reshape(2, LAG_PAD, 2, 128).transpose(2, 1, 0, 3).reshape(2, LAG_PAD, 256)
    blocks = freqs[::8] // 8

    outs = []
    for c in range(CHUNKS):
        rows = slice(c * ROWS, (c + 1) * ROWS)
        outer_a = gather(jnp.concatenate([a[:, rows] for a in inner_a]), shift_x)
        outer_b = gather(jnp.concatenate([a[:, rows] for a in inner_b]), shift_y)
        src = jnp.concatenate(outer_a + outer_b)
        send, keep = correlate(blocks, table, sign, spec, src)
        near = swap_core(send)
        quarter = ROWS // 4
        onward = (keep[:quarter].astype(jnp.float32) + near[:quarter].astype(jnp.float32)).astype(jnp.bfloat16)
        last = swap_far(onward)
        own = keep[quarter:].astype(jnp.float32) + near[quarter:].astype(jnp.float32)
        outs.append((own + last.astype(jnp.float32)).astype(jnp.bfloat16))
    return jnp.concatenate(outs)


def solution(mesh):
    placed = (P("tm", None, None, "chan"), P(), P("tm"))
    return jax.shard_map(
        body, mesh=mesh, in_specs=placed, out_specs=P("tm", None, "chan"), check_vma=False
    )
```

```python
import jax
import jax.numpy as jnp
from jax import lax
from jax.experimental import pallas as pl
from jax.experimental.pallas import tpu as pltpu
from jax.sharding import PartitionSpec as P

LAGS = 101
SRC_BLK = 64
BINS = 250
CHUNKS = 2
ROWS = 128 // CHUNKS
LAG_PAD = 112
STRIDE = 264


def shift_x(x, step):
    pairs = [((a * 4 + b) * 2 + c, (((a + step) % 4) * 4 + b) * 2 + c) for a in range(4) for b in range(4) for c in range(2)]
    return lax.ppermute(x, "chan", pairs)


def shift_y(x, step):
    pairs = [((a * 4 + b) * 2 + c, (a * 4 + (b + step) % 4) * 2 + c) for a in range(4) for b in range(4) for c in range(2)]
    return lax.ppermute(x, "chan", pairs)


def swap_z(x):
    return lax.ppermute(x, "chan", [(a, a ^ 1) for a in range(32)])


def swap_core(x):
    return lax.ppermute(x, "tm", [(a, a ^ 1) for a in range(4)])


def swap_far(x):
    return lax.ppermute(x, "tm", [(a, a ^ 2) for a in range(4)])


def lag_table(freqs, lag_count, segment_total):
    lag_steps = jnp.arange(lag_count, dtype=jnp.int32) - (LAGS - 1) // 2
    phase_int = lag_steps[:, None] * (freqs + 1)[None, :] % (2 * BINS)
    phase = phase_int.astype(jnp.float32) * (2.0 * jnp.pi / (2.0 * BINS))
    scale = 1.0 / jnp.sqrt(jnp.float32(segment_total * BINS))
    both = jnp.stack([jnp.cos(phase) * scale, -jnp.sin(phase) * scale])
    return jnp.where((freqs < BINS)[None, None, :], both, 0.0).astype(jnp.bfloat16)


def pick_kernel(first_ref, pick_ref, mask_ref, spec_a_ref, spec_b_ref, out_a_ref, out_b_ref):
    step = pl.program_id(0)
    for half, (spec_ref, out_ref) in enumerate(((spec_a_ref, out_a_ref), (spec_b_ref, out_b_ref))):
        for w in range(16):
            rows = lax.dot_general(
                pick_ref[...], spec_ref[w], (((1,), (1,)), ((), ())), preferred_element_type=jnp.float32
            )
            kept = jnp.where((first_ref[half] + step) * 16 + w < BINS, rows * mask_ref[...], 0.0)
            out_ref[w] = kept.astype(jnp.bfloat16)


def pick_rows(first, pick, mask, spec):
    part = jax.ShapeDtypeStruct((32, 128, 128), jnp.bfloat16)
    return pl.pallas_call(
        pick_kernel,
        grid_spec=pltpu.PrefetchScalarGridSpec(
            num_scalar_prefetch=1,
            grid=(2,),
            in_specs=[
                pl.BlockSpec((128, 256), lambda i, s: (0, 0)),
                pl.BlockSpec((1, 128), lambda i, s: (0, 0)),
                pl.BlockSpec((16, 128, 256), lambda i, s: (s[0] + i, 0, 0)),
                pl.BlockSpec((16, 128, 256), lambda i, s: (s[1] + i, 0, 0)),
            ],
            out_specs=[pl.BlockSpec((16, 128, 128), lambda i, s: (i, 0, 0))] * 2,
        ),
        out_shape=[part, part],
        compiler_params=pltpu.CompilerParams(vmem_limit_bytes=50 << 20),
        cost_estimate=pl.CostEstimate(flops=4 * 32 * 128 * 128 * 256, bytes_accessed=6 << 20, transcendentals=0),
        name="pick_rows",
    )(first, pick, mask, spec, spec)


def assemble_kernel(at_ref, *refs):
    for e in range(4):
        place = pl.ds(8 * lax.rem(at_ref[0] + 4 - e, 4), 8)
        for c in range(CHUNKS):
            refs[4 + c][place] = refs[e][:, c * ROWS : (c + 1) * ROWS]


def assemble(at, pieces):
    piece = pl.BlockSpec((8, 128, 128), lambda i, s: (0, 0, 0))
    return pl.pallas_call(
        assemble_kernel,
        grid_spec=pltpu.PrefetchScalarGridSpec(
            num_scalar_prefetch=1,
            grid=(1,),
            in_specs=[piece] * 4,
            out_specs=[pl.BlockSpec((32, ROWS, 128), lambda i, s: (0, 0, 0))] * CHUNKS,
        ),
        out_shape=[jax.ShapeDtypeStruct((32, ROWS, 128), jnp.bfloat16)] * CHUNKS,
        compiler_params=pltpu.CompilerParams(vmem_limit_bytes=8 << 20),
        cost_estimate=pl.CostEstimate(flops=0, bytes_accessed=2 << 20, transcendentals=0),
        name="assemble",
    )(at, *pieces)


def correlate_kernel(blocks_ref, table_ref, sign_ref, spec_ref, *refs):
    sources, (send_ref, keep_ref, src, left, right, acc) = refs[:8], refs[8:]
    step = pl.program_id(0)
    for m in range(8):

        @pl.when(step == m)
        def _():
            src[...] = sources[m][...]

    base = lax.rem(step, 4) * 32
    last = BINS - 1 - 32 * blocks_ref[step]
    sign = sign_ref[...]

    @pl.loop(0, 2)
    def _(group):
        for w in range(16):
            i = group * 16 + w
            rows = src[i]
            turned = jnp.concatenate([rows[:, 64:], rows[:, :64]], axis=1) * sign
            both = jnp.concatenate([rows, turned], axis=0)
            cross = jnp.dot(both, spec_ref[jnp.minimum(i, last)], preferred_element_type=jnp.float32)
            for part in range(2):
                place = pl.ds(part * 128 + base + i, ROWS, stride=STRIDE)
                piece = cross[part * ROWS : (part + 1) * ROWS]
                left[place, :] = piece[:, :128]
                right[place, :] = piece[:, 128:]

    def lags(k):
        rows = pl.ds(pl.multiple_of(k * STRIDE, 8), 256)
        cross = jnp.concatenate(
            [left[rows, :].astype(jnp.bfloat16), right[rows, :].astype(jnp.bfloat16)], axis=1
        )
        return jnp.dot(table_ref[0], cross, preferred_element_type=jnp.float32)

    @pl.when(step == 3)
    def _():
        @pl.loop(0, ROWS, step=8)
        def _(first):
            for u in range(8):
                acc[first + u] = lags(first + u)

    @pl.when(step == 7)
    def _():
        @pl.loop(0, ROWS // 2, step=8)
        def _(first):
            for u in range(8):
                k = first + u
                send_ref[k] = (acc[k] + lags(k))[:LAGS].astype(jnp.bfloat16)

        @pl.loop(0, ROWS // 2, step=8)
        def _(first):
            for u in range(8):
                k = first + u + ROWS // 2
                keep_ref[first + u] = (acc[k] + lags(k))[:LAGS].astype(jnp.bfloat16)


def correlate(blocks, table, sign, spec, sources):
    half = jax.ShapeDtypeStruct((ROWS // 2, LAGS, 256), jnp.bfloat16)
    whole = pl.BlockSpec((ROWS // 2, LAGS, 256), lambda i, s: (0, 0, 0))
    return pl.pallas_call(
        correlate_kernel,
        grid_spec=pltpu.PrefetchScalarGridSpec(
            num_scalar_prefetch=1,
            grid=(8,),
            in_specs=[
                pl.BlockSpec((1, LAG_PAD, 256), lambda i, s: (i // 4, 0, 0)),
                pl.BlockSpec((1, 128), lambda i, s: (0, 0)),
                pl.BlockSpec((32, 128, 256), lambda i, s: (s[i], 0, 0)),
            ]
            + [pl.BlockSpec((32, ROWS, 128), lambda i, s: (0, 0, 0))] * 8,
            out_specs=[whole, whole],
            scratch_shapes=[
                pltpu.VMEM((32, ROWS, 128), jnp.bfloat16),
                pltpu.VMEM((ROWS * STRIDE, 128), jnp.float32),
                pltpu.VMEM((ROWS * STRIDE, 128), jnp.float32),
                pltpu.VMEM((ROWS, LAG_PAD, 256), jnp.float32),
            ],
        ),
        out_shape=[half, half],
        compiler_params=pltpu.CompilerParams(vmem_limit_bytes=50 << 20),
        cost_estimate=pl.CostEstimate(flops=20 * 10**9, bytes_accessed=24 << 20, transcendentals=0),
        name="correlate",
    )(blocks, table, sign, spec, *sources)


def body(spectra, src_blocks, valid):
    chan_index = lax.axis_index("chan")
    tm_index = lax.axis_index("tm")
    x, y = chan_index // 8, chan_index // 2 % 4
    core, far = tm_index % 2, tm_index // 2

    spec = jnp.transpose(spectra, (2, 1, 0, 3)).reshape(BINS, 128, 256)

    q = jnp.arange(128, dtype=jnp.int32)
    part, group, within = q // ROWS, q % ROWS // (ROWS // 4), q % (ROWS // 4)
    dest_core = jnp.where(group < 2, 1 - core, core)
    dest_far = jnp.where(group % 2 == 0, 1 - far, far)
    row = 32 * (2 * dest_far + dest_core) + (ROWS // 4) * part + within
    block = jnp.where(row < SRC_BLK, src_blocks[0], src_blocks[1])
    channel = block * SRC_BLK + row % SRC_BLK - chan_index * 256
    pick = (channel[:, None] == jnp.arange(256, dtype=jnp.int32)[None, :]).astype(jnp.bfloat16)
    mask = jnp.tile(valid.astype(jnp.float32), 2)[None, :]
    sign = jnp.where(jnp.arange(128) < 64, -1.0, 1.0).astype(jnp.bfloat16)[None, :]

    own = {d: pick_rows(jnp.stack([2 * ((x + d) % 4), 8 + 2 * ((y + d) % 4)]), pick, mask, spec) for d in (1, 3, 2, 0)}
    quarters_a = [own[0][0]] + [shift_x(own[d][0], d) for d in (1, 3, 2)]
    quarters_b = [own[0][1]] + [shift_y(own[d][1], d) for d in (1, 3, 2)]

    def scatter(quarters, at, shift):
        def piece(d):
            cut = [lax.dynamic_slice_in_dim(a, 8 * ((at + d) % 4), 8, 0) for a in quarters]
            return (cut[0] + cut[1]) + (cut[2] + cut[3])

        got = [shift(piece(d), d) for d in (1, 3, 2)]
        return (piece(0) + got[0]) + (got[1] + got[2])

    piece_a = scatter(quarters_a, y, shift_y)
    piece_b = scatter(quarters_b, x, shift_x)
    piece_a = piece_a + swap_z(piece_a)
    piece_b = piece_b + swap_z(piece_b)

    def gather(a, shift):
        got = {d: shift(a, d) for d in (1, 3, 2)}
        return [a, got[1], got[2], got[3]]

    inner_a = assemble(y[None], gather(piece_a, shift_y))
    inner_b = assemble(x[None], gather(piece_b, shift_x))

    i = jnp.arange(256, dtype=jnp.int32)
    e = i % 128 // 32
    blocks_at = jnp.where(i < 128, (x - e) % 4, 4 + (y - e) % 4)
    table = lag_table(32 * blocks_at + i % 32, LAG_PAD, 256)
    table = table.reshape(2, LAG_PAD, 2, 128).transpose(2, 1, 0, 3).reshape(2, LAG_PAD, 256)
    blocks = blocks_at[::32]

    outs, waiting = [], None
    quarter = ROWS // 4
    arrived = gather(inner_a[0], shift_x) + gather(inner_b[0], shift_y)
    for c in range(CHUNKS):
        following = None
        if c + 1 < CHUNKS:
            following = gather(inner_a[c + 1], shift_x) + gather(inner_b[c + 1], shift_y)
        if waiting is not None:
            last = swap_far(waiting[0])
        send, keep = correlate(blocks, table, sign, spec, arrived)
        if waiting is not None:
            outs.append(finish(waiting, last))
        arrived = following
        near = swap_core(send)
        onward = (keep[:quarter].astype(jnp.float32) + near[:quarter].astype(jnp.float32)).astype(jnp.bfloat16)
        waiting = (onward, keep[quarter:], near[quarter:])
    outs.append(finish(waiting, swap_far(onward)))
    return jnp.concatenate(outs)


def finish(waiting, last):
    own = waiting[1].astype(jnp.float32) + waiting[2].astype(jnp.float32)
    return (own + last.astype(jnp.float32)).astype(jnp.bfloat16)


def solution(mesh):
    placed = (P("tm", None, None, "chan"), P(), P("tm"))
    return jax.shard_map(
        body, mesh=mesh, in_specs=placed, out_specs=P("tm", None, "chan"), check_vma=False
    )
```

```python
import jax
import jax.numpy as jnp
from jax import lax
from jax.experimental import pallas as pl
from jax.experimental.pallas import tpu as pltpu
from jax.sharding import PartitionSpec as P

LAGS = 101
SRC_BLK = 64
BINS = 250
CHUNKS = 2
PARTS = 4
WIDE = 128 // CHUNKS
ROWS = 128 // PARTS
LAG_PAD = 112
LAG = 2
SMALL = pl.CostEstimate(flops=1 << 20, bytes_accessed=1 << 16, transcendentals=0)
STRIDE = 264


def shift_x(x, step):
    pairs = [((a * 4 + b) * 2 + c, (((a + step) % 4) * 4 + b) * 2 + c) for a in range(4) for b in range(4) for c in range(2)]
    return lax.ppermute(x, "chan", pairs)


def shift_y(x, step):
    pairs = [((a * 4 + b) * 2 + c, (a * 4 + (b + step) % 4) * 2 + c) for a in range(4) for b in range(4) for c in range(2)]
    return lax.ppermute(x, "chan", pairs)


def swap_z(x):
    return lax.ppermute(x, "chan", [(a, a ^ 1) for a in range(32)])


def swap_core(x):
    return lax.ppermute(x, "tm", [(a, a ^ 1) for a in range(4)])


def swap_far(x):
    return lax.ppermute(x, "tm", [(a, a ^ 2) for a in range(4)])


def lag_table(freqs, lag_count, segment_total):
    lag_steps = jnp.arange(lag_count, dtype=jnp.int32) - (LAGS - 1) // 2
    phase_int = lag_steps[:, None] * (freqs + 1)[None, :] % (2 * BINS)
    phase = phase_int.astype(jnp.float32) * (2.0 * jnp.pi / (2.0 * BINS))
    scale = 1.0 / jnp.sqrt(jnp.float32(segment_total * BINS))
    both = jnp.stack([jnp.cos(phase) * scale, -jnp.sin(phase) * scale])
    return jnp.where((freqs < BINS)[None, None, :], both, 0.0).astype(jnp.bfloat16)


def pick_kernel(first_ref, pick_ref, mask_ref, spec_a_ref, spec_b_ref, out_a_ref, out_b_ref):
    step = pl.program_id(0)
    for half, (spec_ref, out_ref) in enumerate(((spec_a_ref, out_a_ref), (spec_b_ref, out_b_ref))):
        for w in range(16):
            rows = lax.dot_general(
                pick_ref[...], spec_ref[w], (((1,), (1,)), ((), ())), preferred_element_type=jnp.float32
            )
            kept = jnp.where((first_ref[half] + step) * 16 + w < BINS, rows * mask_ref[...], 0.0)
            out_ref[w] = kept.astype(jnp.bfloat16)


def pick_rows(first, pick, mask, spec):
    part = jax.ShapeDtypeStruct((32, 128, 128), jnp.bfloat16)
    return pl.pallas_call(
        pick_kernel,
        grid_spec=pltpu.PrefetchScalarGridSpec(
            num_scalar_prefetch=1,
            grid=(2,),
            in_specs=[
                pl.BlockSpec((128, 256), lambda i, s: (0, 0)),
                pl.BlockSpec((1, 128), lambda i, s: (0, 0)),
                pl.BlockSpec((16, 128, 256), lambda i, s: (s[0] + i, 0, 0)),
                pl.BlockSpec((16, 128, 256), lambda i, s: (s[1] + i, 0, 0)),
            ],
            out_specs=[pl.BlockSpec((16, 128, 128), lambda i, s: (i, 0, 0))] * 2,
        ),
        out_shape=[part, part],
        compiler_params=pltpu.CompilerParams(vmem_limit_bytes=50 << 20),
        cost_estimate=SMALL,
        name="pick_rows",
    )(first, pick, mask, spec, spec)


def assemble_kernel(at_ref, *refs):
    for e in range(4):
        place = pl.ds(8 * lax.rem(at_ref[0] + 4 - e, 4), 8)
        for c in range(CHUNKS):
            refs[4 + c][place] = refs[e][:, c * WIDE : (c + 1) * WIDE]


def assemble(at, pieces):
    piece = pl.BlockSpec((8, 128, 128), lambda i, s: (0, 0, 0))
    return pl.pallas_call(
        assemble_kernel,
        grid_spec=pltpu.PrefetchScalarGridSpec(
            num_scalar_prefetch=1,
            grid=(1,),
            in_specs=[piece] * 4,
            out_specs=[pl.BlockSpec((32, WIDE, 128), lambda i, s: (0, 0, 0))] * CHUNKS,
        ),
        out_shape=[jax.ShapeDtypeStruct((32, WIDE, 128), jnp.bfloat16)] * CHUNKS,
        compiler_params=pltpu.CompilerParams(vmem_limit_bytes=8 << 20),
        cost_estimate=SMALL,
        name="assemble",
    )(at, *pieces)


def correlate_kernel(blocks_ref, table_ref, sign_ref, spec_ref, *refs):
    sources, (send_ref, keep_ref, src, left, right, acc) = refs[:8], refs[8:]
    step = pl.program_id(0)
    for m in range(8):

        @pl.when(step == m)
        def _():
            src[...] = sources[m][...]

    base = lax.rem(step, 4) * 32
    last = BINS - 1 - 32 * blocks_ref[step]
    sign = sign_ref[...]

    @pl.loop(0, 2)
    def _(group):
        for w in range(16):
            i = group * 16 + w
            rows = src[i]
            turned = jnp.concatenate([rows[:, 64:], rows[:, :64]], axis=1) * sign
            both = jnp.concatenate([rows, turned], axis=0)
            cross = jnp.dot(both, spec_ref[jnp.minimum(i, last)], preferred_element_type=jnp.float32)
            for part in range(2):
                place = pl.ds(part * 128 + base + i, ROWS, stride=STRIDE)
                piece = cross[part * ROWS : (part + 1) * ROWS]
                left[place, :] = piece[:, :128]
                right[place, :] = piece[:, 128:]

    def lags(k):
        rows = pl.ds(pl.multiple_of(k * STRIDE, 8), 256)
        cross = jnp.concatenate(
            [left[rows, :].astype(jnp.bfloat16), right[rows, :].astype(jnp.bfloat16)], axis=1
        )
        return jnp.dot(table_ref[0], cross, preferred_element_type=jnp.float32)

    @pl.when(step == 3)
    def _():
        @pl.loop(0, ROWS, step=8)
        def _(first):
            for u in range(8):
                acc[first + u] = lags(first + u)

    @pl.when(step == 7)
    def _():
        @pl.loop(0, ROWS // 2, step=8)
        def _(first):
            for u in range(8):
                k = first + u
                send_ref[k] = (acc[k] + lags(k))[:LAGS].astype(jnp.bfloat16)

        @pl.loop(0, ROWS // 2, step=8)
        def _(first):
            for u in range(8):
                k = first + u + ROWS // 2
                keep_ref[first + u] = (acc[k] + lags(k))[:LAGS].astype(jnp.bfloat16)


def correlate(part, blocks, table, sign, spec, sources):
    half = jax.ShapeDtypeStruct((ROWS // 2, LAGS, 256), jnp.bfloat16)
    whole = pl.BlockSpec((ROWS // 2, LAGS, 256), lambda i, s: (0, 0, 0))
    return pl.pallas_call(
        correlate_kernel,
        grid_spec=pltpu.PrefetchScalarGridSpec(
            num_scalar_prefetch=1,
            grid=(8,),
            in_specs=[
                pl.BlockSpec((1, LAG_PAD, 256), lambda i, s: (i // 4, 0, 0)),
                pl.BlockSpec((1, 128), lambda i, s: (0, 0)),
                pl.BlockSpec((32, 128, 256), lambda i, s: (s[i], 0, 0)),
            ]
            + [pl.BlockSpec((32, ROWS, 128), lambda i, s: (0, part, 0))] * 8,
            out_specs=[whole, whole],
            scratch_shapes=[
                pltpu.VMEM((32, ROWS, 128), jnp.bfloat16),
                pltpu.VMEM((ROWS * STRIDE, 128), jnp.float32),
                pltpu.VMEM((ROWS * STRIDE, 128), jnp.float32),
                pltpu.VMEM((ROWS, LAG_PAD, 256), jnp.float32),
            ],
        ),
        out_shape=[half, half],
        compiler_params=pltpu.CompilerParams(vmem_limit_bytes=50 << 20),
        cost_estimate=SMALL,
        name="correlate",
    )(blocks, table, sign, spec, *sources)


def body(spectra, src_blocks, valid):
    chan_index = lax.axis_index("chan")
    tm_index = lax.axis_index("tm")
    x, y = chan_index // 8, chan_index // 2 % 4
    core, far = tm_index % 2, tm_index // 2

    spec = jnp.transpose(spectra, (2, 1, 0, 3)).reshape(BINS, 128, 256)

    q = jnp.arange(128, dtype=jnp.int32)
    part, group, within = q // ROWS, q % ROWS // (ROWS // 4), q % (ROWS // 4)
    dest_core = jnp.where(group < 2, 1 - core, core)
    dest_far = jnp.where(group % 2 == 0, 1 - far, far)
    row = 32 * (2 * dest_far + dest_core) + (ROWS // 4) * part + within
    block = jnp.where(row < SRC_BLK, src_blocks[0], src_blocks[1])
    channel = block * SRC_BLK + row % SRC_BLK - chan_index * 256
    pick = (channel[:, None] == jnp.arange(256, dtype=jnp.int32)[None, :]).astype(jnp.bfloat16)
    mask = jnp.tile(valid.astype(jnp.float32), 2)[None, :]
    sign = jnp.where(jnp.arange(128) < 64, -1.0, 1.0).astype(jnp.bfloat16)[None, :]

    barrier = lax.optimization_barrier
    own = {d: pick_rows(jnp.stack([2 * ((x + d) % 4), 8 + 2 * ((y + d) % 4)]), pick, mask, spec) for d in (1, 3, 2, 0)}
    got = {d: (shift_x(own[d][0], d), shift_y(own[d][1], d)) for d in (1, 3, 2)}
    got = barrier(got)

    def piece(half, at, d):
        parts = (own[0][half], got[1][half], got[2][half], got[3][half])
        cut = [lax.dynamic_slice_in_dim(a, 8 * ((at + d) % 4), 8, 0) for a in parts]
        return (cut[0] + cut[1]) + (cut[2] + cut[3])

    pieces = {d: (piece(0, y, d), piece(1, x, d)) for d in range(4)}
    more = barrier({d: (shift_y(pieces[d][0], d), shift_x(pieces[d][1], d)) for d in (1, 3, 2)})
    piece_a, piece_b = [(pieces[0][h] + more[1][h]) + (more[2][h] + more[3][h]) for h in range(2)]
    far_a, far_b = barrier((swap_z(piece_a), swap_z(piece_b)))
    piece_a, piece_b = piece_a + far_a, piece_b + far_b

    def gather(a, b, shift_a, shift_b):
        come = {d: (shift_a(a, d), shift_b(b, d)) for d in (1, 3, 2)}
        come = barrier(come)
        return [a, come[1][0], come[2][0], come[3][0]], [b, come[1][1], come[2][1], come[3][1]]

    near_a, near_b = gather(piece_a, piece_b, shift_y, shift_x)
    inner_a, inner_b = assemble(y[None], near_a), assemble(x[None], near_b)

    i = jnp.arange(256, dtype=jnp.int32)
    e = i % 128 // 32
    blocks_at = jnp.where(i < 128, (x - e) % 4, 4 + (y - e) % 4)
    table = lag_table(32 * blocks_at + i % 32, LAG_PAD, 256)
    table = table.reshape(2, LAG_PAD, 2, 128).transpose(2, 1, 0, 3).reshape(2, LAG_PAD, 256)
    blocks = blocks_at[::32]

    arrivals = []
    for c in range(CHUNKS):
        far_a, far_b = gather(inner_a[c], inner_b[c], shift_x, shift_y)
        arrivals.append(far_a + far_b)
    outs = []
    quarter = ROWS // 4
    for part in range(PARTS):
        at = blocks
        if part >= LAG:
            at, outs[part - LAG] = barrier((blocks, outs[part - LAG]))
        c = part * CHUNKS // PARTS
        send, keep = correlate(part - c * PARTS // CHUNKS, at, table, sign, spec, arrivals[c])
        near = swap_core(send)
        onward = (keep[:quarter].astype(jnp.float32) + near[:quarter].astype(jnp.float32)).astype(jnp.bfloat16)
        outs.append(finish((keep[quarter:], near[quarter:]), swap_far(onward)))
    return jnp.concatenate(outs)


def finish(own_rows, last):
    own = own_rows[0].astype(jnp.float32) + own_rows[1].astype(jnp.float32)
    return (own + last.astype(jnp.float32)).astype(jnp.bfloat16)


def solution(mesh):
    placed = (P("tm", None, None, "chan"), P(), P("tm"))
    return jax.shard_map(
        body, mesh=mesh, in_specs=placed, out_specs=P("tm", None, "chan"), check_vma=False
    )
```

```python
import jax
import jax.numpy as jnp
from jax import lax
from jax.experimental import pallas as pl
from jax.experimental.pallas import tpu as pltpu
from jax.sharding import PartitionSpec as P

LAGS = 101
SRC_BLK = 64
BINS = 250
CHUNKS = 1
PARTS = 2
WIDE = 128 // CHUNKS
ROWS = 128 // PARTS
LAG_PAD = 112
SMALL = pl.CostEstimate(flops=1 << 20, bytes_accessed=1 << 16, transcendentals=0)
STRIDE = 264


def shift_x(x, step):
    pairs = [((a * 4 + b) * 2 + c, (((a + step) % 4) * 4 + b) * 2 + c) for a in range(4) for b in range(4) for c in range(2)]
    return lax.ppermute(x, "chan", pairs)


def shift_y(x, step):
    pairs = [((a * 4 + b) * 2 + c, (a * 4 + (b + step) % 4) * 2 + c) for a in range(4) for b in range(4) for c in range(2)]
    return lax.ppermute(x, "chan", pairs)


def swap_z(x):
    return lax.ppermute(x, "chan", [(a, a ^ 1) for a in range(32)])


def swap_core(x):
    return lax.ppermute(x, "tm", [(a, a ^ 1) for a in range(4)])


def swap_far(x):
    return lax.ppermute(x, "tm", [(a, a ^ 2) for a in range(4)])


def lag_table(freqs, lag_count, segment_total):
    lag_steps = jnp.arange(lag_count, dtype=jnp.int32) - (LAGS - 1) // 2
    phase_int = lag_steps[:, None] * (freqs + 1)[None, :] % (2 * BINS)
    phase = phase_int.astype(jnp.float32) * (2.0 * jnp.pi / (2.0 * BINS))
    scale = 1.0 / jnp.sqrt(jnp.float32(segment_total * BINS))
    both = jnp.stack([jnp.cos(phase) * scale, -jnp.sin(phase) * scale])
    return jnp.where((freqs < BINS)[None, None, :], both, 0.0).astype(jnp.bfloat16)


def pick_kernel(first_ref, pick_ref, mask_ref, spec_a_ref, spec_b_ref, out_a_ref, out_b_ref):
    step = pl.program_id(0)
    for half, (spec_ref, out_ref) in enumerate(((spec_a_ref, out_a_ref), (spec_b_ref, out_b_ref))):
        for w in range(16):
            rows = lax.dot_general(
                pick_ref[...], spec_ref[w], (((1,), (1,)), ((), ())), preferred_element_type=jnp.float32
            )
            kept = jnp.where((first_ref[half] + step) * 16 + w < BINS, rows * mask_ref[...], 0.0)
            out_ref[w] = kept.astype(jnp.bfloat16)


def pick_rows(first, pick, mask, spec):
    part = jax.ShapeDtypeStruct((32, 128, 128), jnp.bfloat16)
    return pl.pallas_call(
        pick_kernel,
        grid_spec=pltpu.PrefetchScalarGridSpec(
            num_scalar_prefetch=1,
            grid=(2,),
            in_specs=[
                pl.BlockSpec((128, 256), lambda i, s: (0, 0)),
                pl.BlockSpec((1, 128), lambda i, s: (0, 0)),
                pl.BlockSpec((16, 128, 256), lambda i, s: (s[0] + i, 0, 0)),
                pl.BlockSpec((16, 128, 256), lambda i, s: (s[1] + i, 0, 0)),
            ],
            out_specs=[pl.BlockSpec((16, 128, 128), lambda i, s: (i, 0, 0))] * 2,
        ),
        out_shape=[part, part],
        compiler_params=pltpu.CompilerParams(vmem_limit_bytes=50 << 20),
        cost_estimate=SMALL,
        name="pick_rows",
    )(first, pick, mask, spec, spec)


def assemble_kernel(at_ref, *refs):
    for e in range(4):
        place = pl.ds(8 * lax.rem(at_ref[0] + 4 - e, 4), 8)
        for c in range(CHUNKS):
            refs[4 + c][place] = refs[e][:, c * WIDE : (c + 1) * WIDE]


def assemble(at, pieces):
    piece = pl.BlockSpec((8, 128, 128), lambda i, s: (0, 0, 0))
    return pl.pallas_call(
        assemble_kernel,
        grid_spec=pltpu.PrefetchScalarGridSpec(
            num_scalar_prefetch=1,
            grid=(1,),
            in_specs=[piece] * 4,
            out_specs=[pl.BlockSpec((32, WIDE, 128), lambda i, s: (0, 0, 0))] * CHUNKS,
        ),
        out_shape=[jax.ShapeDtypeStruct((32, WIDE, 128), jnp.bfloat16)] * CHUNKS,
        compiler_params=pltpu.CompilerParams(vmem_limit_bytes=8 << 20),
        cost_estimate=SMALL,
        name="assemble",
    )(at, *pieces)


def correlate_kernel(blocks_ref, table_ref, sign_ref, spec_ref, *refs):
    sources, (send_ref, keep_ref, src, left, right, acc) = refs[:8], refs[8:]
    step = pl.program_id(0)
    for m in range(8):

        @pl.when(step == m)
        def _():
            src[...] = sources[m][...]

    base = lax.rem(step, 4) * 32
    last = BINS - 1 - 32 * blocks_ref[step]
    sign = sign_ref[...]

    @pl.loop(0, 2)
    def _(group):
        for w in range(16):
            i = group * 16 + w
            rows = src[i]
            turned = jnp.concatenate([rows[:, 64:], rows[:, :64]], axis=1) * sign
            both = jnp.concatenate([rows, turned], axis=0)
            cross = jnp.dot(both, spec_ref[jnp.minimum(i, last)], preferred_element_type=jnp.float32)
            for part in range(2):
                place = pl.ds(part * 128 + base + i, ROWS, stride=STRIDE)
                piece = cross[part * ROWS : (part + 1) * ROWS]
                left[place, :] = piece[:, :128]
                right[place, :] = piece[:, 128:]

    def lags(k):
        rows = pl.ds(pl.multiple_of(k * STRIDE, 8), 256)
        cross = jnp.concatenate(
            [left[rows, :].astype(jnp.bfloat16), right[rows, :].astype(jnp.bfloat16)], axis=1
        )
        return jnp.dot(table_ref[0], cross, preferred_element_type=jnp.float32)

    @pl.when(step == 3)
    def _():
        @pl.loop(0, ROWS, step=8)
        def _(first):
            for u in range(8):
                acc[first + u] = lags(first + u)

    @pl.when(step == 7)
    def _():
        @pl.loop(0, ROWS // 2, step=8)
        def _(first):
            for u in range(8):
                k = first + u
                send_ref[k] = (acc[k] + lags(k))[:LAGS].astype(jnp.bfloat16)

        @pl.loop(0, ROWS // 2, step=8)
        def _(first):
            for u in range(8):
                k = first + u + ROWS // 2
                keep_ref[first + u] = (acc[k] + lags(k))[:LAGS].astype(jnp.bfloat16)


def correlate(part, blocks, table, sign, spec, sources):
    half = jax.ShapeDtypeStruct((ROWS // 2, LAGS, 256), jnp.bfloat16)
    whole = pl.BlockSpec((ROWS // 2, LAGS, 256), lambda i, s: (0, 0, 0))
    return pl.pallas_call(
        correlate_kernel,
        grid_spec=pltpu.PrefetchScalarGridSpec(
            num_scalar_prefetch=1,
            grid=(8,),
            in_specs=[
                pl.BlockSpec((1, LAG_PAD, 256), lambda i, s: (i // 4, 0, 0)),
                pl.BlockSpec((1, 128), lambda i, s: (0, 0)),
                pl.BlockSpec((32, 128, 256), lambda i, s: (s[i], 0, 0)),
            ]
            + [pl.BlockSpec((32, ROWS, 128), lambda i, s: (0, part, 0))] * 8,
            out_specs=[whole, whole],
            scratch_shapes=[
                pltpu.VMEM((32, ROWS, 128), jnp.bfloat16),
                pltpu.VMEM((ROWS * STRIDE, 128), jnp.float32),
                pltpu.VMEM((ROWS * STRIDE, 128), jnp.float32),
                pltpu.VMEM((ROWS, LAG_PAD, 256), jnp.float32),
            ],
        ),
        out_shape=[half, half],
        compiler_params=pltpu.CompilerParams(vmem_limit_bytes=50 << 20),
        cost_estimate=pl.CostEstimate(flops=20 * 10**9, bytes_accessed=24 << 20, transcendentals=0),
        name="correlate",
    )(blocks, table, sign, spec, *sources)


def body(spectra, src_blocks, valid):
    chan_index = lax.axis_index("chan")
    tm_index = lax.axis_index("tm")
    x, y = chan_index // 8, chan_index // 2 % 4
    core, far = tm_index % 2, tm_index // 2

    spec = jnp.transpose(spectra, (2, 1, 0, 3)).reshape(BINS, 128, 256)

    q = jnp.arange(128, dtype=jnp.int32)
    part, group, within = q // ROWS, q % ROWS // (ROWS // 4), q % (ROWS // 4)
    dest_core = jnp.where(group < 2, 1 - core, core)
    dest_far = jnp.where(group % 2 == 0, 1 - far, far)
    row = 32 * (2 * dest_far + dest_core) + (ROWS // 4) * part + within
    block = jnp.where(row < SRC_BLK, src_blocks[0], src_blocks[1])
    channel = block * SRC_BLK + row % SRC_BLK - chan_index * 256
    pick = (channel[:, None] == jnp.arange(256, dtype=jnp.int32)[None, :]).astype(jnp.bfloat16)
    mask = jnp.tile(valid.astype(jnp.float32), 2)[None, :]
    sign = jnp.where(jnp.arange(128) < 64, -1.0, 1.0).astype(jnp.bfloat16)[None, :]

    barrier = lax.optimization_barrier
    own = {d: pick_rows(jnp.stack([2 * ((x + d) % 4), 8 + 2 * ((y + d) % 4)]), pick, mask, spec) for d in (1, 3, 2, 0)}
    got = {d: (shift_x(own[d][0], d), shift_y(own[d][1], d)) for d in (1, 3, 2)}
    got = barrier(got)

    def piece(half, at, d):
        parts = (own[0][half], got[1][half], got[2][half], got[3][half])
        cut = [lax.dynamic_slice_in_dim(a, 8 * ((at + d) % 4), 8, 0) for a in parts]
        return (cut[0] + cut[1]) + (cut[2] + cut[3])

    pieces = {d: (piece(0, y, d), piece(1, x, d)) for d in range(4)}
    more = barrier({d: (shift_y(pieces[d][0], d), shift_x(pieces[d][1], d)) for d in (1, 3, 2)})
    piece_a, piece_b = [(pieces[0][h] + more[1][h]) + (more[2][h] + more[3][h]) for h in range(2)]
    far_a, far_b = barrier((swap_z(piece_a), swap_z(piece_b)))
    piece_a, piece_b = piece_a + far_a, piece_b + far_b

    def gather(a, b, shift_a, shift_b):
        come = {d: (shift_a(a, d), shift_b(b, d)) for d in (1, 3, 2)}
        come = barrier(come)
        return [a, come[1][0], come[2][0], come[3][0]], [b, come[1][1], come[2][1], come[3][1]]

    near_a, near_b = gather(piece_a, piece_b, shift_y, shift_x)
    inner_a, inner_b = assemble(y[None], near_a), assemble(x[None], near_b)

    i = jnp.arange(256, dtype=jnp.int32)
    e = i % 128 // 32
    blocks_at = jnp.where(i < 128, (x - e) % 4, 4 + (y - e) % 4)
    table = lag_table(32 * blocks_at + i % 32, LAG_PAD, 256)
    table = table.reshape(2, LAG_PAD, 2, 128).transpose(2, 1, 0, 3).reshape(2, LAG_PAD, 256)
    blocks = blocks_at[::32]

    arrivals = []
    for c in range(CHUNKS):
        far_a, far_b = gather(inner_a[c], inner_b[c], shift_x, shift_y)
        arrivals.append(far_a + far_b)
    outs = []
    quarter = ROWS // 4
    last = own_rows = None
    for part in range(PARTS):
        c = part * CHUNKS // PARTS
        send, keep = correlate(part - c * PARTS // CHUNKS, blocks, table, sign, spec, arrivals[c])
        if last is not None:
            send, last = barrier((send, last))
            outs.append(finish(own_rows, last))
        near = swap_core(send)
        own_rows = (keep[quarter:], near[quarter:])
        onward = (keep[:quarter].astype(jnp.float32) + near[:quarter].astype(jnp.float32)).astype(jnp.bfloat16)
        last = swap_far(onward)
    outs.append(finish(own_rows, last))
    return jnp.concatenate(outs)


def finish(own_rows, last):
    own = own_rows[0].astype(jnp.float32) + own_rows[1].astype(jnp.float32)
    return (own + last.astype(jnp.float32)).astype(jnp.bfloat16)


def solution(mesh):
    placed = (P("tm", None, None, "chan"), P(), P("tm"))
    return jax.shard_map(
        body, mesh=mesh, in_specs=placed, out_specs=P("tm", None, "chan"), check_vma=False
    )
```

```python
import jax
import jax.numpy as jnp
from jax import lax
from jax.experimental import pallas as pl
from jax.experimental.pallas import tpu as pltpu
from jax.sharding import PartitionSpec as P

LAGS = 101
SRC_BLK = 64
BINS = 250
PARTS = 2
ROWS = 128 // PARTS
LAG_PAD = 112
SMALL = pl.CostEstimate(flops=1 << 20, bytes_accessed=1 << 16, transcendentals=0)
STRIDE = 264


def shift_x(x, step):
    pairs = [((a * 4 + b) * 2 + c, (((a + step) % 4) * 4 + b) * 2 + c) for a in range(4) for b in range(4) for c in range(2)]
    return lax.ppermute(x, "chan", pairs)


def shift_y(x, step):
    pairs = [((a * 4 + b) * 2 + c, (a * 4 + (b + step) % 4) * 2 + c) for a in range(4) for b in range(4) for c in range(2)]
    return lax.ppermute(x, "chan", pairs)


def swap_z(x):
    return lax.ppermute(x, "chan", [(a, a ^ 1) for a in range(32)])


def swap_core(x):
    return lax.ppermute(x, "tm", [(a, a ^ 1) for a in range(4)])


def swap_far(x):
    return lax.ppermute(x, "tm", [(a, a ^ 2) for a in range(4)])


def lag_table(freqs, lag_count, segment_total):
    lag_steps = jnp.arange(lag_count, dtype=jnp.int32) - (LAGS - 1) // 2
    phase_int = lag_steps[:, None] * (freqs + 1)[None, :] % (2 * BINS)
    phase = phase_int.astype(jnp.float32) * (2.0 * jnp.pi / (2.0 * BINS))
    scale = 1.0 / jnp.sqrt(jnp.float32(segment_total * BINS))
    both = jnp.stack([jnp.cos(phase) * scale, -jnp.sin(phase) * scale])
    return jnp.where((freqs < BINS)[None, None, :], both, 0.0).astype(jnp.bfloat16)


def pick_kernel(first_ref, pick_ref, mask_ref, spec_a_ref, spec_b_ref, out_a_ref, out_b_ref):
    step = pl.program_id(0)
    for half, (spec_ref, out_ref) in enumerate(((spec_a_ref, out_a_ref), (spec_b_ref, out_b_ref))):
        for w in range(16):
            rows = lax.dot_general(
                pick_ref[...], spec_ref[w], (((1,), (1,)), ((), ())), preferred_element_type=jnp.float32
            )
            kept = jnp.where((first_ref[half] + step) * 16 + w < BINS, rows * mask_ref[...], 0.0)
            out_ref[w] = kept.astype(jnp.bfloat16)


def pick_rows(first, pick, mask, spec):
    part = jax.ShapeDtypeStruct((32, 128, 128), jnp.bfloat16)
    return pl.pallas_call(
        pick_kernel,
        grid_spec=pltpu.PrefetchScalarGridSpec(
            num_scalar_prefetch=1,
            grid=(2,),
            in_specs=[
                pl.BlockSpec((128, 256), lambda i, s: (0, 0)),
                pl.BlockSpec((1, 128), lambda i, s: (0, 0)),
                pl.BlockSpec((16, 128, 256), lambda i, s: (s[0] + i, 0, 0)),
                pl.BlockSpec((16, 128, 256), lambda i, s: (s[1] + i, 0, 0)),
            ],
            out_specs=[pl.BlockSpec((16, 128, 128), lambda i, s: (i, 0, 0))] * 2,
        ),
        out_shape=[part, part],
        compiler_params=pltpu.CompilerParams(vmem_limit_bytes=50 << 20),
        cost_estimate=SMALL,
        name="pick_rows",
    )(first, pick, mask, spec, spec)


def assemble_kernel(at_ref, *refs):
    for m, e in enumerate((0, 1, 3, 2)):
        place = pl.ds(8 * lax.rem(at_ref[0] + 4 - e, 4), 8)
        refs[4][place] = refs[m][...]


def assemble(at, pieces):
    piece = pl.BlockSpec((8, 128, 128), lambda i, s: (0, 0, 0))
    return pl.pallas_call(
        assemble_kernel,
        grid_spec=pltpu.PrefetchScalarGridSpec(
            num_scalar_prefetch=1,
            grid=(1,),
            in_specs=[piece] * 4,
            out_specs=pl.BlockSpec((32, 128, 128), lambda i, s: (0, 0, 0)),
        ),
        out_shape=jax.ShapeDtypeStruct((32, 128, 128), jnp.bfloat16),
        compiler_params=pltpu.CompilerParams(vmem_limit_bytes=8 << 20),
        cost_estimate=SMALL,
        name="assemble",
    )(at, *pieces)


def cross_blocks(blocks_ref, sign_ref, spec_ref, sources, src, left, right):
    step = pl.program_id(0)
    for m in range(4):

        @pl.when(step == m)
        def _():
            src[...] = sources[m][...]

    last = BINS - 1 - 32 * blocks_ref[step]
    sign = sign_ref[...]

    @pl.loop(0, 2)
    def _(group):
        for w in range(16):
            i = group * 16 + w
            rows = src[i]
            turned = jnp.concatenate([rows[:, 64:], rows[:, :64]], axis=1) * sign
            both = jnp.concatenate([rows, turned], axis=0)
            cross = jnp.dot(both, spec_ref[jnp.minimum(i, last)], preferred_element_type=jnp.float32)
            for part in range(2):
                place = pl.ds(part * 128 + step * 32 + i, ROWS, stride=STRIDE)
                piece = cross[part * ROWS : (part + 1) * ROWS]
                left[place, :] = piece[:, :128]
                right[place, :] = piece[:, 128:]


def lag_sums(k, table_ref, left, right):
    rows = pl.ds(pl.multiple_of(k * STRIDE, 8), 256)
    cross = jnp.concatenate([left[rows, :].astype(jnp.bfloat16), right[rows, :].astype(jnp.bfloat16)], axis=1)
    return jnp.dot(table_ref[...], cross, preferred_element_type=jnp.float32)


def early_kernel(blocks_ref, table_ref, sign_ref, spec_ref, *refs):
    sources, (acc_ref, src, left, right) = refs[:4], refs[4:]
    cross_blocks(blocks_ref, sign_ref, spec_ref, sources, src, left, right)

    @pl.when(pl.program_id(0) == 3)
    def _():
        @pl.loop(0, ROWS, step=8)
        def _(first):
            for u in range(8):
                acc_ref[first + u] = lag_sums(first + u, table_ref, left, right)


def late_kernel(blocks_ref, table_ref, sign_ref, spec_ref, *refs):
    sources, (before_ref, send_ref, keep_ref, src, left, right, acc, sem) = refs[:4], refs[4:]
    step = pl.program_id(0)
    fetch = pltpu.make_async_copy(before_ref, acc, sem)

    @pl.when(step == 0)
    def _():
        fetch.start()

    cross_blocks(blocks_ref, sign_ref, spec_ref, sources, src, left, right)

    @pl.when(step == 3)
    def _():
        fetch.wait()

        @pl.loop(0, ROWS // 2, step=8)
        def _(first):
            for u in range(8):
                k = first + u
                send_ref[k] = (acc[k] + lag_sums(k, table_ref, left, right))[:LAGS].astype(jnp.bfloat16)

        @pl.loop(0, ROWS // 2, step=8)
        def _(first):
            for u in range(8):
                k = first + u + ROWS // 2
                keep_ref[first + u] = (acc[k] + lag_sums(k, table_ref, left, right))[:LAGS].astype(jnp.bfloat16)


def correlate(part, blocks, table, sign, spec, sources, before=None):
    half = jax.ShapeDtypeStruct((ROWS // 2, LAGS, 256), jnp.bfloat16)
    sums = jax.ShapeDtypeStruct((ROWS, LAG_PAD, 256), jnp.float32)
    early = before is None
    whole = pl.BlockSpec((ROWS // 2, LAGS, 256), lambda i, s: (0, 0, 0))
    scratch = [
        pltpu.VMEM((32, ROWS, 128), jnp.bfloat16),
        pltpu.VMEM((ROWS * STRIDE, 128), jnp.float32),
        pltpu.VMEM((ROWS * STRIDE, 128), jnp.float32),
    ]
    if not early:
        scratch += [pltpu.VMEM((ROWS, LAG_PAD, 256), jnp.float32), pltpu.SemaphoreType.DMA]
    return pl.pallas_call(
        early_kernel if early else late_kernel,
        grid_spec=pltpu.PrefetchScalarGridSpec(
            num_scalar_prefetch=1,
            grid=(4,),
            in_specs=[
                pl.BlockSpec((LAG_PAD, 256), lambda i, s: (0, 0)),
                pl.BlockSpec((1, 128), lambda i, s: (0, 0)),
                pl.BlockSpec((32, 128, 256), lambda i, s: (s[i], 0, 0)),
            ]
            + [pl.BlockSpec((32, ROWS, 128), lambda i, s: (0, part, 0))] * 4
            + ([] if early else [pl.BlockSpec(memory_space=pl.ANY)]),
            out_specs=pl.BlockSpec((ROWS, LAG_PAD, 256), lambda i, s: (0, 0, 0)) if early else [whole, whole],
            scratch_shapes=scratch,
        ),
        out_shape=sums if early else [half, half],
        compiler_params=pltpu.CompilerParams(vmem_limit_bytes=46 << 20),
        cost_estimate=pl.CostEstimate(flops=12 * 10**9, bytes_accessed=16 << 20, transcendentals=0),
        name="correlate_early" if early else "correlate_late",
    )(blocks, table, sign, spec, *sources, *([] if early else [before]))


def body(spectra, src_blocks, valid):
    chan_index = lax.axis_index("chan")
    tm_index = lax.axis_index("tm")
    x, y = chan_index // 8, chan_index // 2 % 4
    core, far = tm_index % 2, tm_index // 2

    spec = jnp.transpose(spectra, (2, 1, 0, 3)).reshape(BINS, 128, 256)

    q = jnp.arange(128, dtype=jnp.int32)
    part, group, within = q // ROWS, q % ROWS // (ROWS // 4), q % (ROWS // 4)
    dest_core = jnp.where(group < 2, 1 - core, core)
    dest_far = jnp.where(group % 2 == 0, 1 - far, far)
    row = 32 * (2 * dest_far + dest_core) + (ROWS // 4) * part + within
    block = jnp.where(row < SRC_BLK, src_blocks[0], src_blocks[1])
    channel = block * SRC_BLK + row % SRC_BLK - chan_index * 256
    pick = (channel[:, None] == jnp.arange(256, dtype=jnp.int32)[None, :]).astype(jnp.bfloat16)
    mask = jnp.tile(valid.astype(jnp.float32), 2)[None, :]
    sign = jnp.where(jnp.arange(128) < 64, -1.0, 1.0).astype(jnp.bfloat16)[None, :]

    barrier = lax.optimization_barrier
    own = {d: pick_rows(jnp.stack([2 * ((x + d) % 4), 8 + 2 * ((y + d) % 4)]), pick, mask, spec) for d in (1, 3, 2, 0)}
    got = {d: (shift_x(own[d][0], d), shift_y(own[d][1], d)) for d in (1, 3, 2)}
    got = barrier(got)

    def piece(half, at, d):
        parts = (own[0][half], got[1][half], got[2][half], got[3][half])
        cut = [lax.dynamic_slice_in_dim(a, 8 * ((at + d) % 4), 8, 0) for a in parts]
        return (cut[0] + cut[1]) + (cut[2] + cut[3])

    pieces = {d: (piece(0, y, d), piece(1, x, d)) for d in range(4)}
    more = barrier({d: (shift_y(pieces[d][0], d), shift_x(pieces[d][1], d)) for d in (1, 3, 2)})
    piece_a, piece_b = [(pieces[0][h] + more[1][h]) + (more[2][h] + more[3][h]) for h in range(2)]
    far_a, far_b = barrier((swap_z(piece_a), swap_z(piece_b)))
    piece_a, piece_b = piece_a + far_a, piece_b + far_b

    def gather(a, b, shift_a, shift_b):
        return [a] + [shift_a(a, d) for d in (1, 3, 2)], [b] + [shift_b(b, d) for d in (1, 3, 2)]

    near_a, near_b = gather(piece_a, piece_b, shift_y, shift_x)
    near_a, near_b = barrier((near_a, near_b))
    inner_a, inner_b = assemble(y[None], near_a), assemble(x[None], near_b)

    far_a, far_b = gather(inner_a, inner_b, shift_x, shift_y)
    arrivals = [far_a[0], far_b[0], far_a[1], far_a[2], far_b[1], far_b[2], far_a[3], far_b[3]]
    blocks = jnp.stack(
        [x, 4 + y, (x + 3) % 4, (x + 1) % 4, 4 + (y + 3) % 4, 4 + (y + 1) % 4, (x + 2) % 4, 4 + (y + 2) % 4]
    )
    freqs = (32 * blocks[:, None] + jnp.arange(32, dtype=jnp.int32)[None, :]).reshape(256)
    table = lag_table(freqs, LAG_PAD, 256)
    table = table.reshape(2, LAG_PAD, 2, 128).transpose(2, 1, 0, 3).reshape(2, LAG_PAD, 256)
    sums = [correlate(part, blocks[:4], table[0], sign, spec, arrivals[:4]) for part in range(PARTS)]

    sums = barrier(sums)

    outs = []
    quarter = ROWS // 4
    last = own_rows = None
    for part in range(PARTS):
        send, keep = correlate(part, blocks[4:], table[1], sign, spec, arrivals[4:], sums[part])
        if last is not None:
            send, last = barrier((send, last))
            outs.append(finish(own_rows, last))
        near = swap_core(send)
        own_rows = (keep[quarter:], near[quarter:])
        onward = (keep[:quarter].astype(jnp.float32) + near[:quarter].astype(jnp.float32)).astype(jnp.bfloat16)
        last = swap_far(onward)
    outs.append(finish(own_rows, last))
    return jnp.concatenate(outs)


def finish(own_rows, last):
    own = own_rows[0].astype(jnp.float32) + own_rows[1].astype(jnp.float32)
    return (own + last.astype(jnp.float32)).astype(jnp.bfloat16)


def solution(mesh):
    placed = (P("tm", None, None, "chan"), P(), P("tm"))
    return jax.shard_map(
        body, mesh=mesh, in_specs=placed, out_specs=P("tm", None, "chan"), check_vma=False
    )
```

```python
import jax
import jax.numpy as jnp
from jax import lax
from jax.experimental import pallas as pl
from jax.experimental.pallas import tpu as pltpu
from jax.sharding import PartitionSpec as P

LAGS = 101
SRC_BLK = 64
BINS = 250
PARTS = 2
ROWS = 128 // PARTS
LAG_PAD = 112
SMALL = pl.CostEstimate(flops=1 << 20, bytes_accessed=1 << 16, transcendentals=0)
STRIDE = 264


def shift_x(x, step):
    pairs = [((a * 4 + b) * 2 + c, (((a + step) % 4) * 4 + b) * 2 + c) for a in range(4) for b in range(4) for c in range(2)]
    return lax.ppermute(x, "chan", pairs)


def shift_y(x, step):
    pairs = [((a * 4 + b) * 2 + c, (a * 4 + (b + step) % 4) * 2 + c) for a in range(4) for b in range(4) for c in range(2)]
    return lax.ppermute(x, "chan", pairs)


def swap_z(x):
    return lax.ppermute(x, "chan", [(a, a ^ 1) for a in range(32)])


def swap_core(x):
    return lax.ppermute(x, "tm", [(a, a ^ 1) for a in range(4)])


def swap_far(x):
    return lax.ppermute(x, "tm", [(a, a ^ 2) for a in range(4)])


def lag_table(freqs, lag_count, segment_total):
    lag_steps = jnp.arange(lag_count, dtype=jnp.int32) - (LAGS - 1) // 2
    phase_int = lag_steps[:, None] * (freqs + 1)[None, :] % (2 * BINS)
    phase = phase_int.astype(jnp.float32) * (2.0 * jnp.pi / (2.0 * BINS))
    scale = 1.0 / jnp.sqrt(jnp.float32(segment_total * BINS))
    both = jnp.stack([jnp.cos(phase) * scale, -jnp.sin(phase) * scale])
    return jnp.where((freqs < BINS)[None, None, :], both, 0.0).astype(jnp.bfloat16)


def pick_kernel(first_ref, pick_ref, mask_ref, spec_a_ref, spec_b_ref, out_a_ref, out_b_ref):
    step = pl.program_id(0)
    for half, (spec_ref, out_ref) in enumerate(((spec_a_ref, out_a_ref), (spec_b_ref, out_b_ref))):
        for w in range(16):
            rows = lax.dot_general(
                pick_ref[...], spec_ref[w], (((1,), (1,)), ((), ())), preferred_element_type=jnp.float32
            )
            kept = jnp.where((first_ref[half] + step) * 16 + w < BINS, rows * mask_ref[...], 0.0)
            out_ref[w] = kept.astype(jnp.bfloat16)


def pick_rows(first, pick, mask, spec):
    part = jax.ShapeDtypeStruct((32, 128, 128), jnp.bfloat16)
    return pl.pallas_call(
        pick_kernel,
        grid_spec=pltpu.PrefetchScalarGridSpec(
            num_scalar_prefetch=1,
            grid=(2,),
            in_specs=[
                pl.BlockSpec((128, 256), lambda i, s: (0, 0)),
                pl.BlockSpec((1, 128), lambda i, s: (0, 0)),
                pl.BlockSpec((16, 128, 256), lambda i, s: (s[0] + i, 0, 0)),
                pl.BlockSpec((16, 128, 256), lambda i, s: (s[1] + i, 0, 0)),
            ],
            out_specs=[pl.BlockSpec((16, 128, 128), lambda i, s: (i, 0, 0))] * 2,
        ),
        out_shape=[part, part],
        compiler_params=pltpu.CompilerParams(vmem_limit_bytes=50 << 20),
        cost_estimate=SMALL,
        name="pick_rows",
    )(first, pick, mask, spec, spec)


def assemble_kernel(at_ref, *refs):
    for m, e in enumerate((0, 1, 3, 2)):
        place = pl.ds(8 * lax.rem(at_ref[0] + 4 - e, 4), 8)
        refs[4][place] = refs[m][...]


def assemble(at, pieces):
    piece = pl.BlockSpec((8, 128, 128), lambda i, s: (0, 0, 0))
    return pl.pallas_call(
        assemble_kernel,
        grid_spec=pltpu.PrefetchScalarGridSpec(
            num_scalar_prefetch=1,
            grid=(1,),
            in_specs=[piece] * 4,
            out_specs=pl.BlockSpec((32, 128, 128), lambda i, s: (0, 0, 0)),
        ),
        out_shape=jax.ShapeDtypeStruct((32, 128, 128), jnp.bfloat16),
        compiler_params=pltpu.CompilerParams(vmem_limit_bytes=8 << 20),
        cost_estimate=SMALL,
        name="assemble",
    )(at, *pieces)


def cross_blocks(blocks_ref, sign_ref, spec_ref, sources, src, left, right):
    step = pl.program_id(0)
    for m in range(4):

        @pl.when(step == m)
        def _():
            at = 0
            for piece in sources[m]:
                src[at : at + piece.shape[0]] = piece[...]
                at += piece.shape[0]

    last = BINS - 1 - 32 * blocks_ref[step]
    sign = sign_ref[...]

    @pl.loop(0, 2)
    def _(group):
        for w in range(16):
            i = group * 16 + w
            rows = src[i]
            turned = jnp.concatenate([rows[:, 64:], rows[:, :64]], axis=1) * sign
            both = jnp.concatenate([rows, turned], axis=0)
            cross = jnp.dot(both, spec_ref[jnp.minimum(i, last)], preferred_element_type=jnp.float32)
            for part in range(2):
                place = pl.ds(part * 128 + step * 32 + i, ROWS, stride=STRIDE)
                piece = cross[part * ROWS : (part + 1) * ROWS]
                left[place, :] = piece[:, :128]
                right[place, :] = piece[:, 128:]


def lag_sums(k, table_ref, left, right):
    rows = pl.ds(pl.multiple_of(k * STRIDE, 8), 256)
    cross = jnp.concatenate([left[rows, :].astype(jnp.bfloat16), right[rows, :].astype(jnp.bfloat16)], axis=1)
    return jnp.dot(table_ref[...], cross, preferred_element_type=jnp.float32)


def early_kernel(blocks_ref, table_ref, sign_ref, spec_ref, *refs):
    sources, (acc_ref, src, left, right) = [[r] for r in refs[:4]], refs[4:]
    cross_blocks(blocks_ref, sign_ref, spec_ref, sources, src, left, right)

    @pl.when(pl.program_id(0) == 3)
    def _():
        @pl.loop(0, ROWS, step=8)
        def _(first):
            for u in range(8):
                acc_ref[first + u] = lag_sums(first + u, table_ref, left, right)


def late_kernel(blocks_ref, table_ref, sign_ref, spec_ref, *refs):
    sources = [refs[:1], refs[1:2], refs[2:4], refs[4:6]]
    before_ref, send_ref, keep_ref, src, left, right, acc, sem = refs[6:]
    step = pl.program_id(0)
    fetch = pltpu.make_async_copy(before_ref, acc, sem)

    @pl.when(step == 0)
    def _():
        fetch.start()

    cross_blocks(blocks_ref, sign_ref, spec_ref, sources, src, left, right)

    @pl.when(step == 3)
    def _():
        fetch.wait()

        @pl.loop(0, ROWS // 2, step=8)
        def _(first):
            for u in range(8):
                k = first + u
                send_ref[k] = (acc[k] + lag_sums(k, table_ref, left, right))[:LAGS].astype(jnp.bfloat16)

        @pl.loop(0, ROWS // 2, step=8)
        def _(first):
            for u in range(8):
                k = first + u + ROWS // 2
                keep_ref[first + u] = (acc[k] + lag_sums(k, table_ref, left, right))[:LAGS].astype(jnp.bfloat16)


def correlate(part, blocks, table, sign, spec, sources, before=None):
    half = jax.ShapeDtypeStruct((ROWS // 2, LAGS, 256), jnp.bfloat16)
    sums = jax.ShapeDtypeStruct((ROWS, LAG_PAD, 256), jnp.float32)
    early = before is None
    whole = pl.BlockSpec((ROWS // 2, LAGS, 256), lambda i, s: (0, 0, 0))
    scratch = [
        pltpu.VMEM((32, ROWS, 128), jnp.bfloat16),
        pltpu.VMEM((ROWS * STRIDE, 128), jnp.float32),
        pltpu.VMEM((ROWS * STRIDE, 128), jnp.float32),
    ]
    if not early:
        scratch += [pltpu.VMEM((ROWS, LAG_PAD, 256), jnp.float32), pltpu.SemaphoreType.DMA]
    return pl.pallas_call(
        early_kernel if early else late_kernel,
        grid_spec=pltpu.PrefetchScalarGridSpec(
            num_scalar_prefetch=1,
            grid=(4,),
            in_specs=[
                pl.BlockSpec((LAG_PAD, 256), lambda i, s: (0, 0)),
                pl.BlockSpec((1, 128), lambda i, s: (0, 0)),
                pl.BlockSpec((32, 128, 256), lambda i, s: (s[i], 0, 0)),
            ]
            + [pl.BlockSpec((a.shape[0], ROWS, 128), lambda i, s: (0, part, 0)) for a in sources]
            + ([] if early else [pl.BlockSpec(memory_space=pl.ANY)]),
            out_specs=pl.BlockSpec((ROWS, LAG_PAD, 256), lambda i, s: (0, 0, 0)) if early else [whole, whole],
            scratch_shapes=scratch,
        ),
        out_shape=sums if early else [half, half],
        compiler_params=pltpu.CompilerParams(vmem_limit_bytes=46 << 20),
        cost_estimate=pl.CostEstimate(flops=12 * 10**9, bytes_accessed=16 << 20, transcendentals=0),
        name="correlate_early" if early else "correlate_late",
    )(blocks, table, sign, spec, *sources, *([] if early else [before]))


def body(spectra, src_blocks, valid):
    chan_index = lax.axis_index("chan")
    tm_index = lax.axis_index("tm")
    x, y = chan_index // 8, chan_index // 2 % 4
    core, far = tm_index % 2, tm_index // 2

    spec = jnp.transpose(spectra, (2, 1, 0, 3)).reshape(BINS, 128, 256)

    q = jnp.arange(128, dtype=jnp.int32)
    part, group, within = q // ROWS, q % ROWS // (ROWS // 4), q % (ROWS // 4)
    dest_core = jnp.where(group < 2, 1 - core, core)
    dest_far = jnp.where(group % 2 == 0, 1 - far, far)
    row = 32 * (2 * dest_far + dest_core) + (ROWS // 4) * part + within
    block = jnp.where(row < SRC_BLK, src_blocks[0], src_blocks[1])
    channel = block * SRC_BLK + row % SRC_BLK - chan_index * 256
    pick = (channel[:, None] == jnp.arange(256, dtype=jnp.int32)[None, :]).astype(jnp.bfloat16)
    mask = jnp.tile(valid.astype(jnp.float32), 2)[None, :]
    sign = jnp.where(jnp.arange(128) < 64, -1.0, 1.0).astype(jnp.bfloat16)[None, :]

    barrier = lax.optimization_barrier
    own = {d: pick_rows(jnp.stack([2 * ((x + d) % 4), 8 + 2 * ((y + d) % 4)]), pick, mask, spec) for d in (1, 3, 2, 0)}
    got = {d: (shift_x(own[d][0], d), shift_y(own[d][1], d)) for d in (1, 3, 2)}
    got = barrier(got)

    def piece(half, at, d):
        parts = (own[0][half], got[1][half], got[2][half], got[3][half])
        cut = [lax.dynamic_slice_in_dim(a, 8 * ((at + d) % 4), 8, 0) for a in parts]
        return (cut[0] + cut[1]) + (cut[2] + cut[3])

    pieces = {d: (piece(0, y, d), piece(1, x, d)) for d in range(4)}
    more = barrier({d: (shift_y(pieces[d][0], d), shift_x(pieces[d][1], d)) for d in (1, 3, 2)})
    piece_a, piece_b = [(pieces[0][h] + more[1][h]) + (more[2][h] + more[3][h]) for h in range(2)]
    far_a, far_b = barrier((swap_z(piece_a), swap_z(piece_b)))
    piece_a, piece_b = piece_a + far_a, piece_b + far_b

    def gather(a, b, shift_a, shift_b):
        return [a] + [shift_a(a, d) for d in (1, 3, 2)], [b] + [shift_b(b, d) for d in (1, 3, 2)]

    near_a, near_b = gather(piece_a, piece_b, shift_y, shift_x)
    near_a, near_b = barrier((near_a, near_b))
    inner_a, inner_b = assemble(y[None], near_a), assemble(x[None], near_b)

    next_a = [shift_x(inner_a, 1), shift_x(inner_a, 3)]
    next_b = [shift_y(inner_b, 1), shift_y(inner_b, 3)]
    next_a, next_b = barrier((next_a, next_b))
    over_a = [shift_x(next_a[0][:16], 1), shift_x(next_a[1][16:], 3)]
    over_b = [shift_y(next_b[0][:16], 1), shift_y(next_b[1][16:], 3)]
    first_sources = [inner_a, inner_b] + next_a
    last_sources = next_b + over_a + over_b
    blocks = jnp.stack(
        [x, 4 + y, (x + 3) % 4, (x + 1) % 4, 4 + (y + 3) % 4, 4 + (y + 1) % 4, (x + 2) % 4, 4 + (y + 2) % 4]
    )
    freqs = (32 * blocks[:, None] + jnp.arange(32, dtype=jnp.int32)[None, :]).reshape(256)
    table = lag_table(freqs, LAG_PAD, 256)
    table = table.reshape(2, LAG_PAD, 2, 128).transpose(2, 1, 0, 3).reshape(2, LAG_PAD, 256)
    sums = [correlate(part, blocks[:4], table[0], sign, spec, first_sources) for part in range(PARTS)]

    sums = barrier(sums)

    outs = []
    quarter = ROWS // 4
    last = own_rows = None
    for part in range(PARTS):
        send, keep = correlate(part, blocks[4:], table[1], sign, spec, last_sources, sums[part])
        if last is not None:
            send, last = barrier((send, last))
            outs.append(finish(own_rows, last))
        near = swap_core(send)
        own_rows = (keep[quarter:], near[quarter:])
        onward = (keep[:quarter].astype(jnp.float32) + near[:quarter].astype(jnp.float32)).astype(jnp.bfloat16)
        last = swap_far(onward)
    outs.append(finish(own_rows, last))
    return jnp.concatenate(outs)


def finish(own_rows, last):
    own = own_rows[0].astype(jnp.float32) + own_rows[1].astype(jnp.float32)
    return (own + last.astype(jnp.float32)).astype(jnp.bfloat16)


def solution(mesh):
    placed = (P("tm", None, None, "chan"), P(), P("tm"))
    return jax.shard_map(
        body, mesh=mesh, in_specs=placed, out_specs=P("tm", None, "chan"), check_vma=False
    )
```

```python
import jax
import jax.numpy as jnp
from jax import lax
from jax.experimental import pallas as pl
from jax.experimental.pallas import tpu as pltpu
from jax.sharding import PartitionSpec as P

LAGS = 101
SRC_BLK = 64
BINS = 250
PARTS = 2
ROWS = 128 // PARTS
LAG_PAD = 112
SMALL = pl.CostEstimate(flops=1 << 20, bytes_accessed=1 << 16, transcendentals=0)
STRIDE = 264


def shift_x(x, step):
    pairs = [((a * 4 + b) * 2 + c, (((a + step) % 4) * 4 + b) * 2 + c) for a in range(4) for b in range(4) for c in range(2)]
    return lax.ppermute(x, "chan", pairs)


def shift_y(x, step):
    pairs = [((a * 4 + b) * 2 + c, (a * 4 + (b + step) % 4) * 2 + c) for a in range(4) for b in range(4) for c in range(2)]
    return lax.ppermute(x, "chan", pairs)


def swap_z(x):
    return lax.ppermute(x, "chan", [(a, a ^ 1) for a in range(32)])


def swap_core(x):
    return lax.ppermute(x, "tm", [(a, a ^ 1) for a in range(4)])


def swap_far(x):
    return lax.ppermute(x, "tm", [(a, a ^ 2) for a in range(4)])


def lag_table(freqs, lag_count, segment_total):
    lag_steps = jnp.arange(lag_count, dtype=jnp.int32) - (LAGS - 1) // 2
    phase_int = lag_steps[:, None] * (freqs + 1)[None, :] % (2 * BINS)
    phase = phase_int.astype(jnp.float32) * (2.0 * jnp.pi / (2.0 * BINS))
    scale = 1.0 / jnp.sqrt(jnp.float32(segment_total * BINS))
    both = jnp.stack([jnp.cos(phase) * scale, -jnp.sin(phase) * scale])
    return jnp.where((freqs < BINS)[None, None, :], both, 0.0).astype(jnp.bfloat16)


def pick_kernel(first_ref, pick_ref, mask_ref, spec_a_ref, spec_b_ref, out_a_ref, out_b_ref):
    step = pl.program_id(0)
    for half, (spec_ref, out_ref) in enumerate(((spec_a_ref, out_a_ref), (spec_b_ref, out_b_ref))):
        for w in range(16):
            rows = lax.dot_general(
                pick_ref[...], spec_ref[w], (((1,), (1,)), ((), ())), preferred_element_type=jnp.float32
            )
            kept = jnp.where((first_ref[half] + step) * 16 + w < BINS, rows * mask_ref[...], 0.0)
            out_ref[w] = kept.astype(jnp.bfloat16)


def pick_rows(first, pick, mask, spec):
    part = jax.ShapeDtypeStruct((32, 128, 128), jnp.bfloat16)
    return pl.pallas_call(
        pick_kernel,
        grid_spec=pltpu.PrefetchScalarGridSpec(
            num_scalar_prefetch=1,
            grid=(2,),
            in_specs=[
                pl.BlockSpec((128, 256), lambda i, s: (0, 0)),
                pl.BlockSpec((1, 128), lambda i, s: (0, 0)),
                pl.BlockSpec((16, 128, 256), lambda i, s: (s[0] + i, 0, 0)),
                pl.BlockSpec((16, 128, 256), lambda i, s: (s[1] + i, 0, 0)),
            ],
            out_specs=[pl.BlockSpec((16, 128, 128), lambda i, s: (i, 0, 0))] * 2,
        ),
        out_shape=[part, part],
        compiler_params=pltpu.CompilerParams(vmem_limit_bytes=50 << 20),
        cost_estimate=SMALL,
        name="pick_rows",
    )(first, pick, mask, spec, spec)


def assemble_kernel(at_ref, *refs):
    for m, e in enumerate((0, 1, 3, 2)):
        place = pl.ds(8 * lax.rem(at_ref[0] + 4 - e, 4), 8)
        refs[4][place] = refs[m][...]


def assemble(at, pieces):
    piece = pl.BlockSpec((8, 128, 128), lambda i, s: (0, 0, 0))
    return pl.pallas_call(
        assemble_kernel,
        grid_spec=pltpu.PrefetchScalarGridSpec(
            num_scalar_prefetch=1,
            grid=(1,),
            in_specs=[piece] * 4,
            out_specs=pl.BlockSpec((32, 128, 128), lambda i, s: (0, 0, 0)),
        ),
        out_shape=jax.ShapeDtypeStruct((32, 128, 128), jnp.bfloat16),
        compiler_params=pltpu.CompilerParams(vmem_limit_bytes=8 << 20),
        cost_estimate=SMALL,
        name="assemble",
    )(at, *pieces)


def cross_blocks(blocks_ref, sign_ref, spec_ref, sources, src, left, right):
    step = pl.program_id(0)
    for m in range(len(sources)):

        @pl.when(step == m)
        def _():
            at = 0
            for piece in sources[m]:
                src[at : at + piece.shape[0]] = piece[...]
                at += piece.shape[0]

    last = BINS - 1 - 32 * blocks_ref[step]
    sign = sign_ref[...]

    @pl.loop(0, 2)
    def _(group):
        for w in range(16):
            i = group * 16 + w
            rows = src[i]
            turned = jnp.concatenate([rows[:, 64:], rows[:, :64]], axis=1) * sign
            both = jnp.concatenate([rows, turned], axis=0)
            cross = jnp.dot(both, spec_ref[jnp.minimum(i, last)], preferred_element_type=jnp.float32)
            for part in range(2):
                place = pl.ds(part * 128 + lax.rem(step, 4) * 32 + i, ROWS, stride=STRIDE)
                piece = cross[part * ROWS : (part + 1) * ROWS]
                left[place, :] = piece[:, :128]
                right[place, :] = piece[:, 128:]


def lag_sums(k, table_ref, left, right):
    rows = pl.ds(pl.multiple_of(k * STRIDE, 8), 256)
    cross = jnp.concatenate([left[rows, :].astype(jnp.bfloat16), right[rows, :].astype(jnp.bfloat16)], axis=1)
    return jnp.dot(table_ref[0], cross, preferred_element_type=jnp.float32)


def early_kernel(blocks_ref, table_ref, sign_ref, spec_ref, *refs):
    sources, (acc_ref, src, left, right) = [[r] for r in refs[:4]], refs[4:]
    cross_blocks(blocks_ref, sign_ref, spec_ref, sources, src, left, right)

    @pl.when(pl.program_id(0) == 3)
    def _():
        @pl.loop(0, ROWS, step=8)
        def _(first):
            for u in range(8):
                acc_ref[first + u] = lag_sums(first + u, table_ref, left, right)


def finish_sums(table_ref, left, right, acc, send_ref, keep_ref):
    for start, out_ref in ((0, send_ref), (ROWS // 2, keep_ref)):

        @pl.loop(0, ROWS // 2, step=8)
        def _(first):
            for u in range(8):
                k = first + u + start
                total = acc[k] + lag_sums(k, table_ref, left, right)
                out_ref[first + u] = total[:LAGS].astype(jnp.bfloat16)


def late_kernel(blocks_ref, table_ref, sign_ref, spec_ref, *refs):
    sources = [refs[:1], refs[1:2], refs[2:4], refs[4:6]]
    before_ref, send_ref, keep_ref, src, left, right, acc, sem = refs[6:]
    step = pl.program_id(0)
    fetch = pltpu.make_async_copy(before_ref, acc, sem)

    @pl.when(step == 0)
    def _():
        fetch.start()

    cross_blocks(blocks_ref, sign_ref, spec_ref, sources, src, left, right)

    @pl.when(step == 3)
    def _():
        fetch.wait()
        finish_sums(table_ref, left, right, acc, send_ref, keep_ref)


def whole_kernel(blocks_ref, table_ref, sign_ref, spec_ref, *refs):
    sources = [[r] for r in refs[:6]] + [refs[6:8], refs[8:10]]
    send_ref, keep_ref, src, left, right, acc = refs[10:]
    step = pl.program_id(0)
    cross_blocks(blocks_ref, sign_ref, spec_ref, sources, src, left, right)

    @pl.when(step == 3)
    def _():
        @pl.loop(0, ROWS, step=8)
        def _(first):
            for u in range(8):
                acc[first + u] = lag_sums(first + u, table_ref, left, right)

    @pl.when(step == 7)
    def _():
        finish_sums(table_ref, left, right, acc, send_ref, keep_ref)


def correlate(kernel, part, blocks, table, sign, spec, sources, before=None):
    sums = jax.ShapeDtypeStruct((ROWS, LAG_PAD, 256), jnp.float32)
    half = jax.ShapeDtypeStruct((ROWS // 2, LAGS, 256), jnp.bfloat16)
    sums_block = pl.BlockSpec((ROWS, LAG_PAD, 256), lambda i, s: (0, 0, 0))
    half_block = pl.BlockSpec((ROWS // 2, LAGS, 256), lambda i, s: (0, 0, 0))
    early = kernel is early_kernel
    steps = blocks.shape[0]
    scratch = [
        pltpu.VMEM((32, ROWS, 128), jnp.bfloat16),
        pltpu.VMEM((ROWS * STRIDE, 128), jnp.float32),
        pltpu.VMEM((ROWS * STRIDE, 128), jnp.float32),
    ]
    if not early:
        scratch.append(pltpu.VMEM((ROWS, LAG_PAD, 256), jnp.float32))
    if before is not None:
        scratch.append(pltpu.SemaphoreType.DMA)
    return pl.pallas_call(
        kernel,
        grid_spec=pltpu.PrefetchScalarGridSpec(
            num_scalar_prefetch=1,
            grid=(steps,),
            in_specs=[
                pl.BlockSpec((1, LAG_PAD, 256), lambda i, s: (i // 4, 0, 0)),
                pl.BlockSpec((1, 128), lambda i, s: (0, 0)),
                pl.BlockSpec((32, 128, 256), lambda i, s: (s[i], 0, 0)),
            ]
            + [pl.BlockSpec((a.shape[0], ROWS, 128), lambda i, s: (0, part, 0)) for a in sources]
            + ([] if before is None else [pl.BlockSpec(memory_space=pl.ANY)]),
            out_specs=sums_block if early else [half_block, half_block],
            scratch_shapes=scratch,
        ),
        out_shape=sums if early else [half, half],
        compiler_params=pltpu.CompilerParams(vmem_limit_bytes=50 << 20),
        cost_estimate=pl.CostEstimate(flops=steps * 3 * 10**9, bytes_accessed=steps * (4 << 20), transcendentals=0),
        name=kernel.__name__,
    )(blocks, table, sign, spec, *sources, *([] if before is None else [before]))


def body(spectra, src_blocks, valid):
    chan_index = lax.axis_index("chan")
    tm_index = lax.axis_index("tm")
    x, y = chan_index // 8, chan_index // 2 % 4
    core, far = tm_index % 2, tm_index // 2

    spec = jnp.transpose(spectra, (2, 1, 0, 3)).reshape(BINS, 128, 256)

    q = jnp.arange(128, dtype=jnp.int32)
    part, group, within = q // ROWS, q % ROWS // (ROWS // 4), q % (ROWS // 4)
    dest_core = jnp.where(group < 2, 1 - core, core)
    dest_far = jnp.where(group % 2 == 0, 1 - far, far)
    row = 32 * (2 * dest_far + dest_core) + (ROWS // 4) * part + within
    block = jnp.where(row < SRC_BLK, src_blocks[0], src_blocks[1])
    channel = block * SRC_BLK + row % SRC_BLK - chan_index * 256
    pick = (channel[:, None] == jnp.arange(256, dtype=jnp.int32)[None, :]).astype(jnp.bfloat16)
    mask = jnp.tile(valid.astype(jnp.float32), 2)[None, :]
    sign = jnp.where(jnp.arange(128) < 64, -1.0, 1.0).astype(jnp.bfloat16)[None, :]

    barrier = lax.optimization_barrier
    own = {d: pick_rows(jnp.stack([2 * ((x + d) % 4), 8 + 2 * ((y + d) % 4)]), pick, mask, spec) for d in (1, 3, 2, 0)}
    got = {d: (shift_x(own[d][0], d), shift_y(own[d][1], d)) for d in (1, 3, 2)}
    got = barrier(got)

    def piece(half, at, d):
        parts = (own[0][half], got[1][half], got[2][half], got[3][half])
        cut = [lax.dynamic_slice_in_dim(a, 8 * ((at + d) % 4), 8, 0) for a in parts]
        return (cut[0] + cut[1]) + (cut[2] + cut[3])

    pieces = {d: (piece(0, y, d), piece(1, x, d)) for d in range(4)}
    more = barrier({d: (shift_y(pieces[d][0], d), shift_x(pieces[d][1], d)) for d in (1, 3, 2)})
    piece_a, piece_b = [(pieces[0][h] + more[1][h]) + (more[2][h] + more[3][h]) for h in range(2)]
    far_a, far_b = barrier((swap_z(piece_a), swap_z(piece_b)))
    piece_a, piece_b = piece_a + far_a, piece_b + far_b

    def gather(a, b, shift_a, shift_b):
        return [a] + [shift_a(a, d) for d in (1, 3, 2)], [b] + [shift_b(b, d) for d in (1, 3, 2)]

    near_a, near_b = gather(piece_a, piece_b, shift_y, shift_x)
    near_a, near_b = barrier((near_a, near_b))
    inner_a, inner_b = assemble(y[None], near_a), assemble(x[None], near_b)

    next_a = [shift_x(inner_a, 1), shift_x(inner_a, 3)]
    next_b = [shift_y(inner_b, 1), shift_y(inner_b, 3)]
    next_a, next_b = barrier((next_a, next_b))
    over_a = [shift_x(next_a[0][:16], 1), shift_x(next_a[1][16:], 3)]
    over_b = [shift_y(next_b[0][:16], 1), shift_y(next_b[1][16:], 3)]
    first_sources = [inner_a, inner_b] + next_a
    last_sources = next_b + over_a + over_b
    blocks = jnp.stack(
        [x, 4 + y, (x + 3) % 4, (x + 1) % 4, 4 + (y + 3) % 4, 4 + (y + 1) % 4, (x + 2) % 4, 4 + (y + 2) % 4]
    )
    freqs = (32 * blocks[:, None] + jnp.arange(32, dtype=jnp.int32)[None, :]).reshape(256)
    table = lag_table(freqs, LAG_PAD, 256)
    table = table.reshape(2, LAG_PAD, 2, 128).transpose(2, 1, 0, 3).reshape(2, LAG_PAD, 256)
    sums = correlate(early_kernel, 0, blocks[:4], table[:1], sign, spec, first_sources)

    outs = []
    quarter = ROWS // 4
    last = own_rows = None
    for part in range(PARTS):
        if part == 0:
            send, keep = correlate(late_kernel, 0, blocks[4:], table[1:], sign, spec, last_sources, sums)
        else:
            send, keep = correlate(whole_kernel, part, blocks, table, sign, spec, first_sources + last_sources)
        if last is not None:
            send, last = barrier((send, last))
            outs.append(finish(own_rows, last))
        near = swap_core(send)
        own_rows = (keep[quarter:], near[quarter:])
        onward = (keep[:quarter].astype(jnp.float32) + near[:quarter].astype(jnp.float32)).astype(jnp.bfloat16)
        last = swap_far(onward)
    outs.append(finish(own_rows, last))
    return jnp.concatenate(outs)


def finish(own_rows, last):
    own = own_rows[0].astype(jnp.float32) + own_rows[1].astype(jnp.float32)
    return (own + last.astype(jnp.float32)).astype(jnp.bfloat16)


def solution(mesh):
    placed = (P("tm", None, None, "chan"), P(), P("tm"))
    return jax.shard_map(
        body, mesh=mesh, in_specs=placed, out_specs=P("tm", None, "chan"), check_vma=False
    )
```

```python
import jax
import jax.numpy as jnp
from jax import lax
from jax.experimental import pallas as pl
from jax.experimental.pallas import tpu as pltpu
from jax.sharding import PartitionSpec as P

LAGS = 101
SRC_BLK = 64
BINS = 250
PARTS = 2
ROWS = 128 // PARTS
LAG_PAD = 112
SMALL = pl.CostEstimate(flops=1 << 20, bytes_accessed=1 << 16, transcendentals=0)
STRIDE = 264


def shift_x(x, step):
    pairs = [((a * 4 + b) * 2 + c, (((a + step) % 4) * 4 + b) * 2 + c) for a in range(4) for b in range(4) for c in range(2)]
    return lax.ppermute(x, "chan", pairs)


def shift_y(x, step):
    pairs = [((a * 4 + b) * 2 + c, (a * 4 + (b + step) % 4) * 2 + c) for a in range(4) for b in range(4) for c in range(2)]
    return lax.ppermute(x, "chan", pairs)


def swap_z(x):
    return lax.ppermute(x, "chan", [(a, a ^ 1) for a in range(32)])


def swap_core(x):
    return lax.ppermute(x, "tm", [(a, a ^ 1) for a in range(4)])


def swap_far(x):
    return lax.ppermute(x, "tm", [(a, a ^ 2) for a in range(4)])


def lag_table(freqs, lag_count, segment_total):
    lag_steps = jnp.arange(lag_count, dtype=jnp.int32) - (LAGS - 1) // 2
    phase_int = lag_steps[:, None] * (freqs + 1)[None, :] % (2 * BINS)
    phase = phase_int.astype(jnp.float32) * (2.0 * jnp.pi / (2.0 * BINS))
    scale = 1.0 / jnp.sqrt(jnp.float32(segment_total * BINS))
    both = jnp.stack([jnp.cos(phase) * scale, -jnp.sin(phase) * scale])
    return jnp.where((freqs < BINS)[None, None, :], both, 0.0).astype(jnp.bfloat16)


def pick_kernel(first_ref, pick_ref, mask_ref, spec_a_ref, spec_b_ref, out_a_ref, out_b_ref):
    step = pl.program_id(0)
    for half, (spec_ref, out_ref) in enumerate(((spec_a_ref, out_a_ref), (spec_b_ref, out_b_ref))):
        for w in range(16):
            rows = lax.dot_general(
                pick_ref[...], spec_ref[w], (((1,), (1,)), ((), ())), preferred_element_type=jnp.float32
            )
            kept = jnp.where((first_ref[half] + step) * 16 + w < BINS, rows * mask_ref[...], 0.0)
            out_ref[w] = kept.astype(jnp.bfloat16)


def pick_rows(first, pick, mask, spec):
    part = jax.ShapeDtypeStruct((32, 128, 128), jnp.bfloat16)
    return pl.pallas_call(
        pick_kernel,
        grid_spec=pltpu.PrefetchScalarGridSpec(
            num_scalar_prefetch=1,
            grid=(2,),
            in_specs=[
                pl.BlockSpec((128, 256), lambda i, s: (0, 0)),
                pl.BlockSpec((1, 128), lambda i, s: (0, 0)),
                pl.BlockSpec((16, 128, 256), lambda i, s: (s[0] + i, 0, 0)),
                pl.BlockSpec((16, 128, 256), lambda i, s: (s[1] + i, 0, 0)),
            ],
            out_specs=[pl.BlockSpec((16, 128, 128), lambda i, s: (i, 0, 0))] * 2,
        ),
        out_shape=[part, part],
        compiler_params=pltpu.CompilerParams(vmem_limit_bytes=50 << 20),
        cost_estimate=SMALL,
        name="pick_rows",
    )(first, pick, mask, spec, spec)


def assemble_kernel(at_ref, *refs):
    for m, e in enumerate((0, 1, 3, 2)):
        place = pl.ds(8 * lax.rem(at_ref[0] + 4 - e, 4), 8)
        refs[4][place] = refs[m][...]


def assemble(at, pieces):
    piece = pl.BlockSpec((8, 128, 128), lambda i, s: (0, 0, 0))
    return pl.pallas_call(
        assemble_kernel,
        grid_spec=pltpu.PrefetchScalarGridSpec(
            num_scalar_prefetch=1,
            grid=(1,),
            in_specs=[piece] * 4,
            out_specs=pl.BlockSpec((32, 128, 128), lambda i, s: (0, 0, 0)),
        ),
        out_shape=jax.ShapeDtypeStruct((32, 128, 128), jnp.bfloat16),
        compiler_params=pltpu.CompilerParams(vmem_limit_bytes=8 << 20),
        cost_estimate=SMALL,
        name="assemble",
    )(at, *pieces)


def cross_blocks(blocks_ref, sign_ref, spec_ref, sources, src, left, right):
    step = pl.program_id(0)
    for m in range(len(sources)):

        @pl.when(step == m)
        def _():
            at = 0
            for piece in sources[m]:
                src[at : at + piece.shape[0]] = piece[...]
                at += piece.shape[0]

    last = BINS - 1 - 32 * blocks_ref[step]
    sign = sign_ref[...]

    @pl.loop(0, 2)
    def _(group):
        for w in range(16):
            i = group * 16 + w
            rows = src[i]
            turned = jnp.concatenate([rows[:, 64:], rows[:, :64]], axis=1) * sign
            both = jnp.concatenate([rows, turned], axis=0)
            cross = jnp.dot(both, spec_ref[jnp.minimum(i, last)], preferred_element_type=jnp.float32)
            for part in range(2):
                place = pl.ds(part * 128 + lax.rem(step, 4) * 32 + i, ROWS, stride=STRIDE)
                piece = cross[part * ROWS : (part + 1) * ROWS]
                left[place, :] = piece[:, :128]
                right[place, :] = piece[:, 128:]


def lag_sums(k, table_ref, left, right):
    rows = pl.ds(pl.multiple_of(k * STRIDE, 8), 256)
    cross = jnp.concatenate([left[rows, :].astype(jnp.bfloat16), right[rows, :].astype(jnp.bfloat16)], axis=1)
    return jnp.dot(table_ref[0], cross, preferred_element_type=jnp.float32)


def early_kernel(blocks_ref, table_ref, sign_ref, spec_ref, *refs):
    sources, (acc_ref, src, left, right) = [[r] for r in refs[:4]], refs[4:]
    cross_blocks(blocks_ref, sign_ref, spec_ref, sources, src, left, right)

    @pl.when(pl.program_id(0) == 3)
    def _():
        @pl.loop(0, ROWS, step=8)
        def _(first):
            for u in range(8):
                acc_ref[first + u] = lag_sums(first + u, table_ref, left, right)


def finish_sums(table_ref, left, right, acc, send_ref, keep_ref):
    for start, out_ref in ((0, send_ref), (ROWS // 2, keep_ref)):

        @pl.loop(0, ROWS // 2, step=8)
        def _(first):
            for u in range(8):
                k = first + u + start
                total = acc[k] + lag_sums(k, table_ref, left, right)
                out_ref[first + u] = total[:LAGS].astype(jnp.bfloat16)


def late_kernel(blocks_ref, table_ref, sign_ref, spec_ref, *refs):
    sources = [refs[:1], refs[1:2], refs[2:4], refs[4:6]]
    before_ref, send_ref, keep_ref, src, left, right, acc, sem = refs[6:]
    step = pl.program_id(0)
    fetch = pltpu.make_async_copy(before_ref, acc, sem)

    @pl.when(step == 0)
    def _():
        fetch.start()

    cross_blocks(blocks_ref, sign_ref, spec_ref, sources, src, left, right)

    @pl.when(step == 3)
    def _():
        fetch.wait()
        finish_sums(table_ref, left, right, acc, send_ref, keep_ref)


def whole_kernel(blocks_ref, table_ref, sign_ref, spec_ref, *refs):
    sources = [[r] for r in refs[:6]] + [refs[6:8], refs[8:10]]
    send_ref, keep_ref, src, left, right, acc = refs[10:]
    step = pl.program_id(0)
    cross_blocks(blocks_ref, sign_ref, spec_ref, sources, src, left, right)

    @pl.when(step == 3)
    def _():
        @pl.loop(0, ROWS, step=8)
        def _(first):
            for u in range(8):
                acc[first + u] = lag_sums(first + u, table_ref, left, right)

    @pl.when(step == 7)
    def _():
        finish_sums(table_ref, left, right, acc, send_ref, keep_ref)


def correlate(kernel, part, blocks, table, sign, spec, sources, before=None):
    sums = jax.ShapeDtypeStruct((ROWS, LAG_PAD, 256), jnp.float32)
    half = jax.ShapeDtypeStruct((ROWS // 2, LAGS, 256), jnp.bfloat16)
    sums_block = pl.BlockSpec((ROWS, LAG_PAD, 256), lambda i, s: (0, 0, 0))
    half_block = pl.BlockSpec((ROWS // 2, LAGS, 256), lambda i, s: (0, 0, 0))
    early = kernel is early_kernel
    steps = blocks.shape[0]
    scratch = [
        pltpu.VMEM((32, ROWS, 128), jnp.bfloat16),
        pltpu.VMEM((ROWS * STRIDE, 128), jnp.float32),
        pltpu.VMEM((ROWS * STRIDE, 128), jnp.float32),
    ]
    if not early:
        scratch.append(pltpu.VMEM((ROWS, LAG_PAD, 256), jnp.float32))
    if before is not None:
        scratch.append(pltpu.SemaphoreType.DMA)
    return pl.pallas_call(
        kernel,
        grid_spec=pltpu.PrefetchScalarGridSpec(
            num_scalar_prefetch=1,
            grid=(steps,),
            in_specs=[
                pl.BlockSpec((1, LAG_PAD, 256), lambda i, s: (i // 4, 0, 0)),
                pl.BlockSpec((1, 128), lambda i, s: (0, 0)),
                pl.BlockSpec((32, 128, 256), lambda i, s: (s[i], 0, 0)),
            ]
            + [pl.BlockSpec((a.shape[0], ROWS, 128), lambda i, s: (0, part, 0)) for a in sources]
            + ([] if before is None else [pl.BlockSpec(memory_space=pl.ANY)]),
            out_specs=sums_block if early else [half_block, half_block],
            scratch_shapes=scratch,
        ),
        out_shape=sums if early else [half, half],
        compiler_params=pltpu.CompilerParams(vmem_limit_bytes=50 << 20),
        cost_estimate=pl.CostEstimate(flops=steps * 3 * 10**9, bytes_accessed=steps * (4 << 20), transcendentals=0),
        name=kernel.__name__,
    )(blocks, table, sign, spec, *sources, *([] if before is None else [before]))


def body(spectra, src_blocks, valid):
    chan_index = lax.axis_index("chan")
    tm_index = lax.axis_index("tm")
    x, y = chan_index // 8, chan_index // 2 % 4
    core, far = tm_index % 2, tm_index // 2

    spec = jnp.transpose(spectra, (2, 1, 0, 3)).reshape(BINS, 128, 256)

    q = jnp.arange(128, dtype=jnp.int32)
    part, group, within = q // ROWS, q % ROWS // (ROWS // 4), q % (ROWS // 4)
    dest_core = jnp.where(group < 2, 1 - core, core)
    dest_far = jnp.where(group % 2 == 0, 1 - far, far)
    row = 32 * (2 * dest_far + dest_core) + (ROWS // 4) * part + within
    block = jnp.where(row < SRC_BLK, src_blocks[0], src_blocks[1])
    channel = block * SRC_BLK + row % SRC_BLK - chan_index * 256
    pick = (channel[:, None] == jnp.arange(256, dtype=jnp.int32)[None, :]).astype(jnp.bfloat16)
    mask = jnp.tile(valid.astype(jnp.float32), 2)[None, :]
    sign = jnp.where(jnp.arange(128) < 64, -1.0, 1.0).astype(jnp.bfloat16)[None, :]

    barrier = lax.optimization_barrier
    own = {}
    for d, before in ((1, None), (2, 1), (3, 2), (0, 3)):
        first = jnp.stack([2 * ((x + d) % 4), 8 + 2 * ((y + d) % 4)])
        if before is not None:
            first, own[before] = barrier((first, own[before]))
        own[d] = pick_rows(first, pick, mask, spec)
    got = {d: (shift_x(own[d][0], d), shift_y(own[d][1], d)) for d in (1, 3, 2)}
    got = barrier(got)

    def piece(half, at, d):
        parts = (own[0][half], got[1][half], got[2][half], got[3][half])
        cut = [lax.dynamic_slice_in_dim(a, 8 * ((at + d) % 4), 8, 0) for a in parts]
        return (cut[0] + cut[1]) + (cut[2] + cut[3])

    pieces = {d: (piece(0, y, d), piece(1, x, d)) for d in range(4)}
    more = barrier({d: (shift_y(pieces[d][0], d), shift_x(pieces[d][1], d)) for d in (1, 3, 2)})
    piece_a, piece_b = [(pieces[0][h] + more[1][h]) + (more[2][h] + more[3][h]) for h in range(2)]
    far_a, far_b = barrier((swap_z(piece_a), swap_z(piece_b)))
    piece_a, piece_b = piece_a + far_a, piece_b + far_b

    def gather(a, b, shift_a, shift_b):
        return [a] + [shift_a(a, d) for d in (1, 3, 2)], [b] + [shift_b(b, d) for d in (1, 3, 2)]

    near_a, near_b = gather(piece_a, piece_b, shift_y, shift_x)
    near_a, near_b = barrier((near_a, near_b))
    inner_a, inner_b = assemble(y[None], near_a), assemble(x[None], near_b)

    next_a = [shift_x(inner_a, 1), shift_x(inner_a, 3)]
    next_b = [shift_y(inner_b, 1), shift_y(inner_b, 3)]
    next_a, next_b = barrier((next_a, next_b))
    over_a = [shift_x(next_a[0][:16], 1), shift_x(next_a[1][16:], 3)]
    over_b = [shift_y(next_b[0][:16], 1), shift_y(next_b[1][16:], 3)]
    first_sources = [inner_a, inner_b] + next_a
    last_sources = next_b + over_a + over_b
    blocks = jnp.stack(
        [x, 4 + y, (x + 3) % 4, (x + 1) % 4, 4 + (y + 3) % 4, 4 + (y + 1) % 4, (x + 2) % 4, 4 + (y + 2) % 4]
    )
    freqs = (32 * blocks[:, None] + jnp.arange(32, dtype=jnp.int32)[None, :]).reshape(256)
    table = lag_table(freqs, LAG_PAD, 256)
    table = table.reshape(2, LAG_PAD, 2, 128).transpose(2, 1, 0, 3).reshape(2, LAG_PAD, 256)
    sums = correlate(early_kernel, 0, blocks[:4], table[:1], sign, spec, first_sources)

    outs = []
    quarter = ROWS // 4
    last = own_rows = None
    for part in range(PARTS):
        if part == 0:
            send, keep = correlate(late_kernel, 0, blocks[4:], table[1:], sign, spec, last_sources, sums)
        else:
            send, keep = correlate(whole_kernel, part, blocks, table, sign, spec, first_sources + last_sources)
        if last is not None:
            send, last = barrier((send, last))
            outs.append(finish(own_rows, last))
        near = swap_core(send)
        own_rows = (keep[quarter:], near[quarter:])
        onward = (keep[:quarter].astype(jnp.float32) + near[:quarter].astype(jnp.float32)).astype(jnp.bfloat16)
        last = swap_far(onward)
    outs.append(finish(own_rows, last))
    return jnp.concatenate(outs)


def finish(own_rows, last):
    own = own_rows[0].astype(jnp.float32) + own_rows[1].astype(jnp.float32)
    return (own + last.astype(jnp.float32)).astype(jnp.bfloat16)


def solution(mesh):
    placed = (P("tm", None, None, "chan"), P(), P("tm"))
    return jax.shard_map(
        body, mesh=mesh, in_specs=placed, out_specs=P("tm", None, "chan"), check_vma=False
    )
```

```python
import jax
import jax.numpy as jnp
from jax import lax
from jax.experimental import pallas as pl
from jax.experimental.pallas import tpu as pltpu
from jax.sharding import PartitionSpec as P

LAGS = 101
SRC_BLK = 64
BINS = 250
PARTS = 2
ROWS = 128 // PARTS
LAG_PAD = 112
SMALL = pl.CostEstimate(flops=1 << 20, bytes_accessed=1 << 16, transcendentals=0)
STRIDE = 264


def shift_x(x, step):
    pairs = [((a * 4 + b) * 2 + c, (((a + step) % 4) * 4 + b) * 2 + c) for a in range(4) for b in range(4) for c in range(2)]
    return lax.ppermute(x, "chan", pairs)


def shift_y(x, step):
    pairs = [((a * 4 + b) * 2 + c, (a * 4 + (b + step) % 4) * 2 + c) for a in range(4) for b in range(4) for c in range(2)]
    return lax.ppermute(x, "chan", pairs)


def swap_z(x):
    return lax.ppermute(x, "chan", [(a, a ^ 1) for a in range(32)])


def swap_core(x):
    return lax.ppermute(x, "tm", [(a, a ^ 1) for a in range(4)])


def swap_far(x):
    return lax.ppermute(x, "tm", [(a, a ^ 2) for a in range(4)])


def lag_table(freqs, lag_count, segment_total):
    lag_steps = jnp.arange(lag_count, dtype=jnp.int32) - (LAGS - 1) // 2
    phase_int = lag_steps[:, None] * (freqs + 1)[None, :] % (2 * BINS)
    phase = phase_int.astype(jnp.float32) * (2.0 * jnp.pi / (2.0 * BINS))
    scale = 1.0 / jnp.sqrt(jnp.float32(segment_total * BINS))
    both = jnp.stack([jnp.cos(phase) * scale, -jnp.sin(phase) * scale])
    return jnp.where((freqs < BINS)[None, None, :], both, 0.0).astype(jnp.bfloat16)


def pick_kernel(first_ref, pick_ref, mask_ref, spec_a_ref, spec_b_ref, out_a_ref, out_b_ref):
    step = pl.program_id(0)
    for half, (spec_ref, out_ref) in enumerate(((spec_a_ref, out_a_ref), (spec_b_ref, out_b_ref))):
        for w in range(16):
            rows = lax.dot_general(
                pick_ref[...], spec_ref[w], (((1,), (1,)), ((), ())), preferred_element_type=jnp.float32
            )
            kept = jnp.where((first_ref[half] + step) * 16 + w < BINS, rows * mask_ref[...], 0.0)
            out_ref[w] = kept.astype(jnp.bfloat16)


def pick_rows(first, pick, mask, spec):
    part = jax.ShapeDtypeStruct((32, 128, 128), jnp.bfloat16)
    return pl.pallas_call(
        pick_kernel,
        grid_spec=pltpu.PrefetchScalarGridSpec(
            num_scalar_prefetch=1,
            grid=(2,),
            in_specs=[
                pl.BlockSpec((128, 256), lambda i, s: (0, 0)),
                pl.BlockSpec((1, 128), lambda i, s: (0, 0)),
                pl.BlockSpec((16, 128, 256), lambda i, s: (s[0] + i, 0, 0)),
                pl.BlockSpec((16, 128, 256), lambda i, s: (s[1] + i, 0, 0)),
            ],
            out_specs=[pl.BlockSpec((16, 128, 128), lambda i, s: (i, 0, 0))] * 2,
        ),
        out_shape=[part, part],
        compiler_params=pltpu.CompilerParams(vmem_limit_bytes=50 << 20),
        cost_estimate=SMALL,
        name="pick_rows",
    )(first, pick, mask, spec, spec)


def assemble_kernel(at_ref, *refs):
    for m, e in enumerate((0, 1, 3, 2)):
        place = pl.ds(8 * lax.rem(at_ref[0] + 4 - e, 4), 8)
        refs[4][place] = refs[m][...]


def assemble(at, pieces):
    piece = pl.BlockSpec((8, 128, 128), lambda i, s: (0, 0, 0))
    return pl.pallas_call(
        assemble_kernel,
        grid_spec=pltpu.PrefetchScalarGridSpec(
            num_scalar_prefetch=1,
            grid=(1,),
            in_specs=[piece] * 4,
            out_specs=pl.BlockSpec((32, 128, 128), lambda i, s: (0, 0, 0)),
        ),
        out_shape=jax.ShapeDtypeStruct((32, 128, 128), jnp.bfloat16),
        compiler_params=pltpu.CompilerParams(vmem_limit_bytes=8 << 20),
        cost_estimate=SMALL,
        name="assemble",
    )(at, *pieces)


def cross_blocks(blocks_ref, sign_ref, spec_ref, sources, src, left, right):
    step = pl.program_id(0)
    for m in range(len(sources)):

        @pl.when(step == m)
        def _():
            at = 0
            for piece in sources[m]:
                src[at : at + piece.shape[0]] = piece[...]
                at += piece.shape[0]

    last = BINS - 1 - 32 * blocks_ref[step]
    sign = sign_ref[...]

    @pl.loop(0, 2)
    def _(group):
        for w in range(16):
            i = group * 16 + w
            rows = src[i]
            turned = jnp.concatenate([rows[:, 64:], rows[:, :64]], axis=1) * sign
            both = jnp.concatenate([rows, turned], axis=0)
            cross = jnp.dot(both, spec_ref[jnp.minimum(i, last)], preferred_element_type=jnp.float32)
            for part in range(2):
                place = pl.ds(part * 128 + lax.rem(step, 4) * 32 + i, ROWS, stride=STRIDE)
                piece = cross[part * ROWS : (part + 1) * ROWS]
                left[place, :] = piece[:, :128]
                right[place, :] = piece[:, 128:]


def lag_sums(k, table_ref, left, right):
    rows = pl.ds(pl.multiple_of(k * STRIDE, 8), 256)
    cross = jnp.concatenate([left[rows, :].astype(jnp.bfloat16), right[rows, :].astype(jnp.bfloat16)], axis=1)
    return jnp.dot(table_ref[0], cross, preferred_element_type=jnp.float32)


def early_kernel(blocks_ref, table_ref, sign_ref, spec_ref, *refs):
    sources, (acc_ref, src, left, right) = [[r] for r in refs[:4]], refs[4:]
    cross_blocks(blocks_ref, sign_ref, spec_ref, sources, src, left, right)

    @pl.when(pl.program_id(0) == 3)
    def _():
        @pl.loop(0, ROWS, step=8)
        def _(first):
            for u in range(8):
                acc_ref[first + u] = lag_sums(first + u, table_ref, left, right)


def finish_sums(table_ref, left, right, acc, send_ref, keep_ref):
    for start, out_ref in ((0, send_ref), (ROWS // 2, keep_ref)):

        @pl.loop(0, ROWS // 2, step=8)
        def _(first):
            for u in range(8):
                k = first + u + start
                total = acc[k] + lag_sums(k, table_ref, left, right)
                out_ref[first + u] = total[:LAGS].astype(jnp.bfloat16)


def late_kernel(blocks_ref, table_ref, sign_ref, spec_ref, *refs):
    sources = [refs[:1], refs[1:2], refs[2:4], refs[4:6]]
    before_ref, send_ref, keep_ref, src, left, right, acc, sem = refs[6:]
    step = pl.program_id(0)
    fetch = pltpu.make_async_copy(before_ref, acc, sem)

    @pl.when(step == 0)
    def _():
        fetch.start()

    cross_blocks(blocks_ref, sign_ref, spec_ref, sources, src, left, right)

    @pl.when(step == 3)
    def _():
        fetch.wait()
        finish_sums(table_ref, left, right, acc, send_ref, keep_ref)


def whole_kernel(blocks_ref, table_ref, sign_ref, spec_ref, *refs):
    sources = [[r] for r in refs[:6]] + [refs[6:8], refs[8:10]]
    send_ref, keep_ref, src, left, right, acc = refs[10:]
    step = pl.program_id(0)
    cross_blocks(blocks_ref, sign_ref, spec_ref, sources, src, left, right)

    @pl.when(step == 3)
    def _():
        @pl.loop(0, ROWS, step=8)
        def _(first):
            for u in range(8):
                acc[first + u] = lag_sums(first + u, table_ref, left, right)

    @pl.when(step == 7)
    def _():
        finish_sums(table_ref, left, right, acc, send_ref, keep_ref)


def correlate(kernel, part, blocks, table, sign, spec, sources, before=None):
    sums = jax.ShapeDtypeStruct((ROWS, LAG_PAD, 256), jnp.float32)
    half = jax.ShapeDtypeStruct((ROWS // 2, LAGS, 256), jnp.bfloat16)
    sums_block = pl.BlockSpec((ROWS, LAG_PAD, 256), lambda i, s: (0, 0, 0))
    half_block = pl.BlockSpec((ROWS // 2, LAGS, 256), lambda i, s: (0, 0, 0))
    early = kernel is early_kernel
    steps = blocks.shape[0]
    scratch = [
        pltpu.VMEM((32, ROWS, 128), jnp.bfloat16),
        pltpu.VMEM((ROWS * STRIDE, 128), jnp.float32),
        pltpu.VMEM((ROWS * STRIDE, 128), jnp.float32),
    ]
    if not early:
        scratch.append(pltpu.VMEM((ROWS, LAG_PAD, 256), jnp.float32))
    if before is not None:
        scratch.append(pltpu.SemaphoreType.DMA)
    return pl.pallas_call(
        kernel,
        grid_spec=pltpu.PrefetchScalarGridSpec(
            num_scalar_prefetch=1,
            grid=(steps,),
            in_specs=[
                pl.BlockSpec((1, LAG_PAD, 256), lambda i, s: (i // 4, 0, 0)),
                pl.BlockSpec((1, 128), lambda i, s: (0, 0)),
                pl.BlockSpec((32, 128, 256), lambda i, s: (s[i], 0, 0)),
            ]
            + [pl.BlockSpec((a.shape[0], ROWS, 128), lambda i, s: (0, part, 0)) for a in sources]
            + ([] if before is None else [pl.BlockSpec(memory_space=pl.ANY)]),
            out_specs=sums_block if early else [half_block, half_block],
            scratch_shapes=scratch,
        ),
        out_shape=sums if early else [half, half],
        compiler_params=pltpu.CompilerParams(vmem_limit_bytes=50 << 20),
        cost_estimate=pl.CostEstimate(flops=steps * 3 * 10**9, bytes_accessed=steps * (4 << 20), transcendentals=0),
        name=kernel.__name__,
    )(blocks, table, sign, spec, *sources, *([] if before is None else [before]))


def body(spectra, src_blocks, valid):
    chan_index = lax.axis_index("chan")
    tm_index = lax.axis_index("tm")
    x, y = chan_index // 8, chan_index // 2 % 4
    core, far = tm_index % 2, tm_index // 2

    spec = jnp.transpose(spectra, (2, 1, 0, 3)).reshape(BINS, 128, 256)

    q = jnp.arange(128, dtype=jnp.int32)
    part, group, within = q // ROWS, q % ROWS // (ROWS // 4), q % (ROWS // 4)
    dest_core = jnp.where(group < 2, 1 - core, core)
    dest_far = jnp.where(group % 2 == 0, 1 - far, far)
    row = 32 * (2 * dest_far + dest_core) + (ROWS // 4) * part + within
    block = jnp.where(row < SRC_BLK, src_blocks[0], src_blocks[1])
    channel = block * SRC_BLK + row % SRC_BLK - chan_index * 256
    pick = (channel[:, None] == jnp.arange(256, dtype=jnp.int32)[None, :]).astype(jnp.bfloat16)
    mask = jnp.tile(valid.astype(jnp.float32), 2)[None, :]
    sign = jnp.where(jnp.arange(128) < 64, -1.0, 1.0).astype(jnp.bfloat16)[None, :]

    barrier = lax.optimization_barrier
    own = {}
    for d, before in ((1, None), (2, 1), (3, 2), (0, 3)):
        first = jnp.stack([2 * ((x + d) % 4), 8 + 2 * ((y + d) % 4)])
        if before is not None:
            first, own[before] = barrier((first, own[before]))
        own[d] = pick_rows(first, pick, mask, spec)
    got = {d: (shift_x(own[d][0], d), shift_y(own[d][1], d)) for d in (1, 3, 2)}
    got = barrier(got)

    def piece(half, at, d):
        parts = (own[0][half], got[1][half], got[2][half], got[3][half])
        cut = [lax.dynamic_slice_in_dim(a, 8 * ((at + d) % 4), 8, 0) for a in parts]
        return (cut[0] + cut[1]) + (cut[2] + cut[3])

    pieces = {d: (piece(0, y, d), piece(1, x, d)) for d in range(4)}
    more = barrier({d: (shift_y(pieces[d][0], d), shift_x(pieces[d][1], d)) for d in (1, 3, 2)})
    piece_a, piece_b = [(pieces[0][h] + more[1][h]) + (more[2][h] + more[3][h]) for h in range(2)]
    far_a, far_b = swap_z(piece_a), swap_z(piece_b)
    piece_a, piece_b = piece_a + far_a, piece_b + far_b

    def gather(a, b, shift_a, shift_b):
        return [a] + [shift_a(a, d) for d in (1, 3, 2)], [b] + [shift_b(b, d) for d in (1, 3, 2)]

    near_a, near_b = gather(piece_a, piece_b, shift_y, shift_x)
    near_a, near_b = barrier((near_a, near_b))
    inner_a, inner_b = assemble(y[None], near_a), assemble(x[None], near_b)

    next_a = [shift_x(inner_a, 1), shift_x(inner_a, 3)]
    next_b = [shift_y(inner_b, 1), shift_y(inner_b, 3)]
    next_a, next_b = barrier((next_a, next_b))
    over_a = [shift_x(next_a[0][:16], 1), shift_x(next_a[1][16:], 3)]
    over_b = [shift_y(next_b[0][:16], 1), shift_y(next_b[1][16:], 3)]
    first_sources = [inner_a, inner_b] + next_a
    last_sources = next_b + over_a + over_b
    blocks = jnp.stack(
        [x, 4 + y, (x + 3) % 4, (x + 1) % 4, 4 + (y + 3) % 4, 4 + (y + 1) % 4, (x + 2) % 4, 4 + (y + 2) % 4]
    )
    freqs = (32 * blocks[:, None] + jnp.arange(32, dtype=jnp.int32)[None, :]).reshape(256)
    table = lag_table(freqs, LAG_PAD, 256)
    table = table.reshape(2, LAG_PAD, 2, 128).transpose(2, 1, 0, 3).reshape(2, LAG_PAD, 256)
    sums = correlate(early_kernel, 0, blocks[:4], table[:1], sign, spec, first_sources)

    outs = []
    quarter = ROWS // 4
    last = own_rows = None
    for part in range(PARTS):
        if part == 0:
            send, keep = correlate(late_kernel, 0, blocks[4:], table[1:], sign, spec, last_sources, sums)
        else:
            send, keep = correlate(whole_kernel, part, blocks, table, sign, spec, first_sources + last_sources)
        if last is not None:
            send, last = barrier((send, last))
            outs.append(finish(own_rows, last))
        near = swap_core(send)
        own_rows = (keep[quarter:], near[quarter:])
        onward = (keep[:quarter].astype(jnp.float32) + near[:quarter].astype(jnp.float32)).astype(jnp.bfloat16)
        last = swap_far(onward)
    outs.append(finish(own_rows, last))
    return jnp.concatenate(outs)


def finish(own_rows, last):
    own = own_rows[0].astype(jnp.float32) + own_rows[1].astype(jnp.float32)
    return (own + last.astype(jnp.float32)).astype(jnp.bfloat16)


def solution(mesh):
    placed = (P("tm", None, None, "chan"), P(), P("tm"))
    return jax.shard_map(
        body, mesh=mesh, in_specs=placed, out_specs=P("tm", None, "chan"), check_vma=False
    )
```
